256 devices in a mesh: blk: 16 (over x, y_lo, core), lane: 16 (over y_hi, z).
Axes of the slice: x: 4, y: 4 (y_hi: 2, y_lo: 2; y = y_hi * 2 + y_lo), z: 8, core: 2. Of those that a mesh axis runs over, the one named last changes fastest.
Arguments:
- recv_pos: float32 [3, 32768], P(None, ('blk', 'lane')), may hold values from 0 to 6
- recv_angles: float32 [2, 32768], P(None, ('blk', 'lane')), may hold values from -3.140625 to 3.140625
- src_pos: float32 [3, 262144], P(None, ('blk', 'lane')), may hold values from 0 to 6
- src_angles: float32 [2, 262144], P(None, ('blk', 'lane')), may hold values from -3.140625 to 3.140625
- src_area: float32 [262144], P(('blk', 'lane')), may hold values from 0.02 to 0.08
- reemission: float32 [262144], P(('blk', 'lane')), may hold values from 0.1 to 0.9
- incident: bfloat16 [262144, 128], P(('blk', 'lane')), may hold values from 0 to 2
- direct: float32 [32768, 128], P(('blk', 'lane')), may hold values from 0.5 to 1.5
- visible_lists: int32 [16, 16, 16, 16, 4], P('blk', 'lane'), may hold values from 0 to 7, as said below
- visible_counts: int32 [16, 16, 16, 16], P('blk', 'lane'), may hold values from 0 to 4, as said below
Outputs:
- incoming: float32 [32768, 128], P(('blk', 'lane'))
The draws below stay inside these ranges and needn't reach their ends.
Inputs may be any that keep to these rules, and one draw needn't show every extreme that they name: `visible_lists`: each list names 4 different local source blocks of its device; entries at slots at or past the count are valid but unused. `visible_counts`: some list holds exactly 4 used entries in every draw; the loads differ from device to device.
All inputs are finite; a program needn't handle non-finite values.
Results may differ from the reference program's by a relative error of at most 0.0003.
Values sent between devices are 32-bit elements; how exact they have to be, the bound alone decides.
No kernel may reach another device: no remote copies, remote signals or barrier semaphores. Data moves between devices by JAX's collectives and lax.ppermute only.
A program may use at most 64 MiB of HBM per device.

```python
import math
import jax
import jax.numpy as jnp
from jax import lax

BS = 128
BINS = 128
SB_DEV = 8
CAP = 4
NR = 32768
NS = 262144
N_BLK = 16
N_LANE = 16


def draw_visible_lists(key, part):
    total_lists = N_BLK * N_LANE * N_BLK * N_LANE
    streams = jax.random.split(jax.random.fold_in(key, 11), total_lists)
    picked = jax.vmap(lambda stream: jax.random.permutation(stream, SB_DEV)[:CAP])(streams)
    picked = picked.reshape(N_BLK, N_LANE, N_BLK, N_LANE, CAP).astype(jnp.int32)
    return picked.at[0, 0, 0, 0, :].set((SB_DEV - 1 - jnp.arange(CAP)).astype(jnp.int32))


def draw_visible_counts(key, part):
    first_key, second_key = jax.random.split(jax.random.fold_in(key, 12))
    weight = jax.random.randint(first_key, (N_BLK, N_LANE, 1, 1), 0, 4)
    drawn = jax.random.randint(second_key, (N_BLK, N_LANE, N_BLK, N_LANE), 0, 3 * weight + 1)
    counts = jnp.minimum(drawn, CAP).astype(jnp.int32)
    return counts.at[0, 0, :, 0].set(CAP)


def level_of(key, shape, cuts, least, high):
    def one(position, shards_of):
        steps = jax.random.uniform(jax.random.fold_in(jax.random.fold_in(key, 6), position), (shards_of,), jnp.float32, least / len(cuts), high / len(cuts))
        return jnp.repeat(jnp.exp(steps), shape[position] // shards_of).reshape((-1,) + (1,) * (len(shape) - position - 1))

    gain = one(*cuts[0])
    for cut in cuts[1:]:
        gain = gain * one(*cut)
    return gain


def setup_inputs(seed: int = 0) -> dict:
    splits = jax.random.split(jax.random.key(seed), 11)
    recv_pos = jnp.clip(6.0 * jax.random.uniform(splits[0], (3, NR), jnp.float32) ** level_of(splits[0], (3, NR), ((1, 256),), -0.2, 0.2), 0.0, 6.0)
    recv_angles = jnp.clip(jax.random.uniform(splits[1], (2, NR), jnp.float32, -3.140625, 3.140625), -3.140625, 3.140625)
    src_pos = jnp.clip(6.0 * jax.random.uniform(splits[2], (3, NS), jnp.float32) ** level_of(splits[2], (3, NS), ((1, 256),), -0.2, 0.2), 0.0, 6.0)
    src_angles = jnp.clip(jax.random.uniform(splits[3], (2, NS), jnp.float32, -3.140625, 3.140625), -3.140625, 3.140625)
    src_area = jnp.clip(jnp.exp(math.log(0.08) - 1.3862944 * jax.random.uniform(splits[4], (NS,), jnp.float32) ** level_of(splits[4], (NS,), ((0, 256),), -0.2, 0.2)), 0.02, 0.08)
    reemission = jnp.clip(0.1 + 0.79999997 * jax.random.uniform(splits[5], (NS,), jnp.float32) ** level_of(splits[5], (NS,), ((0, 256),), -0.2, 0.2), 0.1, 0.9)
    incident = jnp.clip(2.0 * jax.random.uniform(splits[6], (NS, BINS), jnp.float32) ** level_of(splits[6], (NS, BINS), ((0, 256),), -0.2, 0.2), 0.0, 2.0).astype(jnp.bfloat16)
    direct = jnp.clip(0.5 + 1.0 * jax.random.uniform(splits[7], (NR, BINS), jnp.float32) ** level_of(splits[7], (NR, BINS), ((0, 256),), -0.2, 0.2), 0.5, 1.5)
    visible_lists = draw_visible_lists(jax.random.fold_in(splits[10], 71), 0)
    visible_counts = draw_visible_counts(jax.random.fold_in(splits[10], 71), 0)
    return {"recv_pos": recv_pos, "recv_angles": recv_angles, "src_pos": src_pos, "src_angles": src_angles, "src_area": src_area, "reemission": reemission, "incident": incident, "direct": direct, "visible_lists": visible_lists, "visible_counts": visible_counts}


def normals(angle_rows):
    polar = angle_rows[0]
    azimuth = angle_rows[1]
    return jnp.stack([jnp.sin(polar) * jnp.cos(azimuth), jnp.sin(polar) * jnp.sin(azimuth), jnp.cos(polar)])


def factors(receiver_pos, receiver_dir, source_pos, source_dir, source_area, source_keep):
    offsets = [source_pos[component] - receiver_pos[component] for component in range(3)]
    distance = offsets[0] * offsets[0] + offsets[1] * offsets[1] + offsets[2] * offsets[2]
    facing = jnp.maximum(receiver_dir[0] * offsets[0] + receiver_dir[1] * offsets[1] + receiver_dir[2] * offsets[2], 0.0)
    seen = jnp.maximum(-(source_dir[0] * offsets[0] + source_dir[1] * offsets[1] + source_dir[2] * offsets[2]), 0.0)
    spread = distance + source_area
    value = source_keep * source_area * facing * seen / (jnp.pi * spread * spread)
    return value.astype(jnp.bfloat16)


def reference(recv_pos, recv_angles, src_pos, src_angles, src_area, reemission, incident, direct, visible_lists, visible_counts):
    device_count = N_BLK * N_LANE
    receiver_pos = recv_pos.reshape(3, N_BLK, N_LANE, BS)
    receiver_dir = normals(recv_angles).reshape(3, N_BLK, N_LANE, BS)
    source_pos = src_pos.reshape(3, device_count, SB_DEV, BS)
    source_dir = normals(src_angles).reshape(3, device_count, SB_DEV, BS)
    source_area = src_area.reshape(device_count, SB_DEV, BS)
    source_keep = reemission.reshape(device_count, SB_DEV, BS)
    emission = incident.reshape(device_count, SB_DEV, BS, BINS)
    all_lists = visible_lists.reshape(device_count, N_BLK, N_LANE, CAP)
    all_counts = visible_counts.reshape(device_count, N_BLK, N_LANE)
    slot_range = jnp.arange(CAP, dtype=jnp.int32)

    def one_device(totals, device):
        chosen = all_lists[device]
        counts_here = all_counts[device]
        picked_pos = source_pos[:, device][:, chosen]
        picked_dir = source_dir[:, device][:, chosen]
        picked_area = source_area[device][chosen]
        picked_keep = source_keep[device][chosen]
        picked_flux = emission[device][chosen]
        values = factors(receiver_pos[:, :, :, :, None, None], receiver_dir[:, :, :, :, None, None],
                         picked_pos[:, :, :, None, :, :], picked_dir[:, :, :, None, :, :],
                         picked_area[:, :, None, :, :], picked_keep[:, :, None, :, :])
        live_mask = (slot_range[None, None, :] < counts_here[:, :, None])[:, :, None, :, None]
        values = jnp.where(live_mask, values, jnp.zeros((), jnp.bfloat16))
        gained = jnp.einsum('gjrcs,gjcsb->gjrb', values.astype(jnp.float32), picked_flux.astype(jnp.float32))
        return totals + gained.reshape(N_BLK * N_LANE * BS, BINS), None

    start = jnp.zeros((N_BLK * N_LANE * BS, BINS), jnp.float32)
    totals, unused = lax.scan(one_device, start, jnp.arange(device_count, dtype=jnp.int32))
    return direct + totals
```

```python
import functools

import jax
import jax.numpy as jnp
import numpy as np
from jax import lax
from jax.experimental import pallas as pl
from jax.experimental.pallas import tpu as pltpu
from jax.sharding import Mesh
from jax.sharding import PartitionSpec as P

NX, NYL, NC, NYH, NZ = 4, 2, 2, 2, 8
NY = NYL * NYH
BS = 128
SB = 8
CAP = 4
GROUP = NX * NC
NJ = NY * NZ
NULL = GROUP * SB
CENTRE = 3.0
ROWS = 16
POS, NRM, DOT, SQA, SQB, ONE, LST = 0, 3, 6, 7, 8, 9, 10
KF, KS, KD = 32, 32, 48
UNROLL = 8


def selection_matrices():
    pieces = [(i, j) for i in range(3) for j in range(3) if i + j < 4]

    def build(depth, terms):
        recv = np.zeros((depth, 3 * ROWS), np.float32)
        src = np.zeros((depth, 3 * ROWS), np.float32)
        for at, (scale, ri, rrow, si, srow) in enumerate(terms):
            recv[at, ri * ROWS + rrow] = scale
            src[at, si * ROWS + srow] = 1.0
        return recv, src

    def product(scale, rrow, srow):
        return [(scale, i, rrow + a, j, srow + a) for i, j in pieces for a in range(3)]

    def from_recv(row, count):
        return [(1.0, i, row, 0, ONE) for i in range(count)]

    def from_src(row, count):
        return [(1.0, 0, ONE, i, row) for i in range(count)]

    facing = product(1.0, NRM, POS) + from_recv(DOT, 3)
    seen = product(1.0, POS, NRM) + from_src(DOT, 3)
    cross = product(-2.0, POS, POS)
    spread = (
        from_recv(SQA, 2) + from_src(SQA, 2) + cross + from_recv(SQB, 3) + from_src(SQB, 3)
    )
    return [build(KF, facing), build(KS, seen), build(KD, spread)]


def null_spread():
    column = np.zeros((KD, BS), np.float32)
    column[2, :] = 1.0
    return column


def split_pieces(tile):
    row = lax.broadcasted_iota(jnp.int32, tile.shape, 0)
    fixed = row < NRM
    high = jnp.where(fixed, jnp.round(tile * 32.0) * (1.0 / 32.0), tile).astype(jnp.bfloat16)
    rest = tile - high.astype(jnp.float32)
    mid = jnp.where(fixed, jnp.round(rest * 8192.0) * (1.0 / 8192.0), rest).astype(jnp.bfloat16)
    low = (rest - mid.astype(jnp.float32)).astype(jnp.bfloat16)
    return jnp.concatenate([high, mid, low], axis=0)


def dot(a, b):
    return jnp.dot(a, b, preferred_element_type=jnp.float32)


def recv_prep_kernel(tiles, mf, ms, md, rf, rs, rd):
    def one(j, carry):
        y, z = j // NZ, j % NZ
        at = (y % NYL) * (NYH * NZ) + (y // NYL) * NZ + z
        q = split_pieces(tiles[at])
        for m, out in ((mf, rf), (ms, rs), (md, rd)):
            out[j] = lax.dot_general(
                q, m[...], (((0,), (1,)), ((), ())), preferred_element_type=jnp.float32
            ).astype(jnp.bfloat16)
        return carry

    lax.fori_loop(0, NJ, one, 0)


def src_prep_kernel(*refs):
    packed = refs[:GROUP]
    mf, ms, md, nul, sf, ss, sd, em = refs[GROUP:]
    for d in range(GROUP):
        ref = packed[d]

        def one(k, carry, ref=ref, d=d):
            start = pl.multiple_of(k * BS, BS)
            em[d * SB + k] = ref[pl.ds(start, BS), :].astype(jnp.bfloat16)
            tile_at = pl.multiple_of(SB * BS + k * ROWS, ROWS)
            q = split_pieces(ref[pl.ds(tile_at, ROWS), :])
            for m, out in ((mf, sf), (ms, ss), (md, sd)):
                out[d * SB + k] = dot(m[...], q).astype(jnp.bfloat16)
            return carry

        lax.fori_loop(0, SB, one, 0)
    em[NULL] = jnp.zeros((BS, BS), jnp.bfloat16)
    sf[NULL] = jnp.zeros((KF, BS), jnp.bfloat16)
    ss[NULL] = jnp.zeros((KS, BS), jnp.bfloat16)
    sd[NULL] = nul[...]


def sweep_kernel(first, lists, rf, rs, rd, sf, ss, sd, em, out, ids, owner):
    base = first[0]
    out[...] = jnp.zeros(out.shape, out.dtype)

    def one_block(j, n):
        def one_entry(t, n):
            value = lists[(t // CAP) * BS + (base + j) * CAP + t % CAP]
            ids[n] = (t // CAP) * SB + value
            owner[n // 2] = j
            return n + (value >= 0).astype(jnp.int32)

        n = lax.fori_loop(0, GROUP * CAP, one_entry, n, unroll=8)
        ids[n] = NULL
        return n + n % 2

    n = lax.fori_loop(0, NZ, one_block, 0)

    def pad(t, carry):
        ids[n + t] = NULL
        owner[(n + t) // 2] = 0
        return carry

    lax.fori_loop(0, 2 * UNROLL, pad, 0, unroll=True)

    def front(u):
        a, b = ids[2 * u], ids[2 * u + 1]
        j = base + owner[u]

        def pair(ref):
            return jnp.concatenate([ref[a], ref[b]], axis=1)

        facing = jnp.maximum(dot(rf[j], pair(sf)), 0.0)
        seen = jnp.maximum(dot(rs[j], pair(ss)), 0.0)
        spread = dot(rd[j], pair(sd))
        return (facing * seen / (spread * spread)).astype(jnp.bfloat16)

    def back(u, values):
        a, b = ids[2 * u], ids[2 * u + 1]
        j = owner[u]
        out[j] = out[j] + dot(values, jnp.concatenate([em[a], em[b]], axis=0))

    def step(i, carry):
        values = [front(i * UNROLL + r) for r in range(UNROLL)]
        for r in range(UNROLL):
            back(i * UNROLL + r, values[r])
        return carry

    lax.fori_loop(0, pl.cdiv(n // 2, UNROLL), step, 0)


VMEM_SPEC = pl.BlockSpec(memory_space=pltpu.VMEM)
SMEM_SPEC = pl.BlockSpec(memory_space=pltpu.SMEM)
BF16 = jnp.bfloat16


def bf16_shape(*shape):
    return jax.ShapeDtypeStruct(shape, BF16)


def recv_prep(tiles, mats):
    return pl.pallas_call(
        recv_prep_kernel,
        out_shape=[bf16_shape(NJ, BS, KF), bf16_shape(NJ, BS, KS), bf16_shape(NJ, BS, KD)],
        in_specs=[VMEM_SPEC] * 4,
        out_specs=[VMEM_SPEC] * 3,
        name="recv_prep",
        cost_estimate=pl.CostEstimate(flops=10**7, bytes_accessed=4 * 10**6, transcendentals=0),
    )(tiles, *mats)


def src_prep(packed, mats, nul):
    return pl.pallas_call(
        src_prep_kernel,
        out_shape=[
            bf16_shape(NULL + 1, KF, BS),
            bf16_shape(NULL + 1, KS, BS),
            bf16_shape(NULL + 1, KD, BS),
            bf16_shape(NULL + 1, BS, BS),
        ],
        in_specs=[VMEM_SPEC] * (GROUP + 4),
        out_specs=[VMEM_SPEC] * 4,
        name="src_prep",
        cost_estimate=pl.CostEstimate(flops=10**7, bytes_accessed=9 * 10**6, transcendentals=0),
    )(*packed, *mats, nul)


def sweep(first, lists, recv, src):
    return pl.pallas_call(
        sweep_kernel,
        out_shape=jax.ShapeDtypeStruct((NZ, BS, BS), jnp.float32),
        in_specs=[SMEM_SPEC] * 2 + [VMEM_SPEC] * 7,
        out_specs=VMEM_SPEC,
        scratch_shapes=[
            pltpu.SMEM((NZ * GROUP * CAP + 4 * UNROLL,), jnp.int32),
            pltpu.SMEM((NZ * GROUP * CAP // 2 + 2 * UNROLL,), jnp.int32),
        ],
        name="sweep",
        cost_estimate=pl.CostEstimate(
            flops=4 * 10**9, bytes_accessed=8 * 10**6, transcendentals=2 * 10**6
        ),
    )(first, lists, *recv, *src)


def normals(angle_rows):
    polar = angle_rows[0]
    azimuth = angle_rows[1]
    return jnp.stack(
        [jnp.sin(polar) * jnp.cos(azimuth), jnp.sin(polar) * jnp.sin(azimuth), jnp.cos(polar)]
    )


def base_rows(pos, direction, extra):
    centred = pos - CENTRE
    coarse = jnp.round(centred * 32.0) * (1.0 / 32.0)
    fine = centred - coarse
    square_a = coarse[0] * coarse[0] + coarse[1] * coarse[1] + coarse[2] * coarse[2]
    square_b = (
        fine[0] * (2.0 * coarse[0] + fine[0])
        + fine[1] * (2.0 * coarse[1] + fine[1])
        + fine[2] * (2.0 * coarse[2] + fine[2])
    ) + extra
    along = -(
        direction[0] * centred[0] + direction[1] * centred[1] + direction[2] * centred[2]
    )
    rows = [centred, direction, along[None], square_a[None], square_b[None]]
    return jnp.concatenate(rows + [jnp.ones_like(along)[None]], axis=0)


def y_route(distance):
    def linear(y):
        return (y % NYL) * NYH + y // NYL

    return [(linear(y), linear((y + distance) % NY)) for y in range(NY)]


def shards(
    recv_pos,
    recv_angles,
    src_pos,
    src_angles,
    src_area,
    reemission,
    incident,
    direct,
    visible_lists,
    visible_counts,
):
    mats = selection_matrices()
    recv_mats = [jnp.asarray(r, BF16) for r, _ in mats]
    src_mats = [jnp.asarray(s, BF16) for _, s in mats]
    nul = jnp.asarray(null_spread(), BF16)

    scale = reemission * src_area * (1.0 / np.pi)
    rows = base_rows(src_pos, normals(src_angles) * scale, src_area)
    rows = rows.reshape(LST, SB, BS).transpose(1, 0, 2)
    slots = jnp.arange(CAP, dtype=jnp.int32)
    live = slots < visible_counts[0, 0][:, :, None]
    marked = jnp.where(live, visible_lists[0, 0], -1)
    marked = marked.reshape(NX, NYL, NC, NYH, NZ, CAP).transpose(0, 2, 3, 1, 4, 5)
    marked = marked.reshape(GROUP, 1, NJ * CAP).astype(jnp.float32)
    rest = jnp.zeros((SB, ROWS - LST - 1, BS), jnp.float32)
    tiles = jnp.concatenate([rows, marked, rest], axis=1).reshape(SB * ROWS, BS)
    mine = jnp.concatenate([incident.astype(jnp.float32), tiles], axis=0)

    def along_x(block, distance):
        return lax.ppermute(block, "x", [(i, (i + distance) % NX) for i in range(NX)])

    def other_core(block):
        return lax.ppermute(block, "c", [(0, 1), (1, 0)])

    gathered = [mine] + [along_x(mine, d) for d in (1, 3, 2)]
    gathered = gathered + [other_core(block) for block in gathered]

    recv_rows = base_rows(recv_pos, normals(recv_angles), jnp.zeros((BS,), jnp.float32))
    recv_tile = jnp.concatenate([recv_rows, jnp.zeros((ROWS - LST, BS), jnp.float32)], axis=0)
    recv_tiles = lax.all_to_all(
        jnp.broadcast_to(recv_tile, (NJ, ROWS, BS)), ("yl", "yh", "z"), 0, 0, tiled=True
    )
    recv = recv_prep(recv_tiles, recv_mats)

    src = src_prep(gathered, src_mats, nul)
    me = lax.axis_index("x") * NC + lax.axis_index("c")
    at = SB * BS + me * ROWS + LST
    lists = jnp.concatenate(
        [lax.dynamic_slice(block, (at, 0), (1, BS)) for block in gathered], axis=0
    )
    lists = lists.astype(jnp.int32).reshape(GROUP * BS)

    y = lax.axis_index("yh") * NYL + lax.axis_index("yl")

    def chunk(distance):
        target = (y + distance) % NY
        return sweep((target * NZ).astype(jnp.int32).reshape(1), lists, recv, src)

    def along_y(block, distance):
        return lax.ppermute(block, ("yl", "yh"), y_route(distance))

    arrived = [along_y(chunk(d), d) for d in (2, 1, 3)]
    total = chunk(0) + arrived[0] + arrived[1] + arrived[2]
    pieces = lax.all_to_all(total, "z", 0, 0, tiled=True)
    return direct + jnp.sum(pieces, axis=0)


def solution(mesh):
    fine = Mesh(mesh.devices.reshape(NX, NYL, NC, NYH, NZ), ("x", "yl", "c", "yh", "z"))
    blk, lane = ("x", "yl", "c"), ("yh", "z")
    both = blk + lane
    return jax.shard_map(
        shards,
        mesh=fine,
        in_specs=(
            P(None, both),
            P(None, both),
            P(None, both),
            P(None, both),
            P(both),
            P(both),
            P(both, None),
            P(both, None),
            P(blk, lane, None, None, None),
            P(blk, lane, None, None),
        ),
        out_specs=P(both, None),
        check_vma=False,
    )
```

```python
import functools

import jax
import jax.numpy as jnp
import numpy as np
from jax import lax
from jax.experimental import pallas as pl
from jax.experimental.pallas import tpu as pltpu
from jax.sharding import Mesh
from jax.sharding import PartitionSpec as P

NX, NYL, NC, NYH, NZ = 4, 2, 2, 2, 8
NY = NYL * NYH
BS = 128
SB = 8
CAP = 4
GROUP = NX * NC
NJ = NY * NZ
CENTRE = 3.0
ROWS = 16
POS, NRM, DOT, SQA, SQB, ONE, LST = 0, 3, 6, 7, 8, 9, 10
KF, KS, KD = 32, 32, 48
VMEM_LIMIT = 24 << 20
UNROLL = 8


def selection_matrices():
    pieces = [(i, j) for i in range(3) for j in range(3) if i + j < 4]

    def build(depth, terms):
        recv = np.zeros((depth, 3 * ROWS), np.float32)
        src = np.zeros((depth, 3 * ROWS), np.float32)
        for at, (scale, ri, rrow, si, srow) in enumerate(terms):
            recv[at, ri * ROWS + rrow] = scale
            src[at, si * ROWS + srow] = 1.0
        return recv, src

    def product(scale, rrow, srow):
        return [(scale, i, rrow + a, j, srow + a) for i, j in pieces for a in range(3)]

    def from_recv(row, count):
        return [(1.0, i, row, 0, ONE) for i in range(count)]

    def from_src(row, count):
        return [(1.0, 0, ONE, i, row) for i in range(count)]

    facing = product(1.0, NRM, POS) + from_recv(DOT, 3)
    seen = product(1.0, POS, NRM) + from_src(DOT, 3)
    cross = product(-2.0, POS, POS)
    spread = (
        from_recv(SQA, 2) + from_src(SQA, 2) + cross + from_recv(SQB, 3) + from_src(SQB, 3)
    )
    return [build(KF, facing), build(KS, seen), build(KD, spread)]


def null_spread():
    column = np.zeros((KD, BS), np.float32)
    column[2, :] = 1.0
    return column


def split_pieces(tile):
    row = lax.broadcasted_iota(jnp.int32, tile.shape, 0)
    fixed = row < NRM
    high = jnp.where(fixed, jnp.round(tile * 32.0) * (1.0 / 32.0), tile).astype(jnp.bfloat16)
    rest = tile - high.astype(jnp.float32)
    mid = jnp.where(fixed, jnp.round(rest * 8192.0) * (1.0 / 8192.0), rest).astype(jnp.bfloat16)
    low = (rest - mid.astype(jnp.float32)).astype(jnp.bfloat16)
    return jnp.concatenate([high, mid, low], axis=0)


def dot(a, b):
    return jnp.dot(a, b, preferred_element_type=jnp.float32)


def src_prep_kernel(count, me, *refs):
    packed = refs[:count]
    mf, ms, md, nul, sf, ss, sd, em, lists = refs[count:]
    list_at = SB * BS + me[0] * ROWS + LST
    for d in range(count):
        ref = packed[d]
        for k in range(SB):
            em[d * SB + k] = ref[k * BS : (k + 1) * BS, :].astype(jnp.bfloat16)
        tiles = [ref[SB * BS + k * ROWS : SB * BS + (k + 1) * ROWS, :] for k in range(SB)]
        q = split_pieces(jnp.concatenate(tiles, axis=1))
        lists[d : d + 1, :] = ref[pl.ds(list_at, 1), :].astype(jnp.int32)
        for m, out in ((mf, sf), (ms, ss), (md, sd)):
            values = dot(m[...], q).astype(jnp.bfloat16)
            for k in range(SB):
                out[d * SB + k] = values[:, k * BS : (k + 1) * BS]
    null = count * SB
    em[null] = jnp.zeros((BS, BS), jnp.bfloat16)
    sf[null] = jnp.zeros((KF, BS), jnp.bfloat16)
    ss[null] = jnp.zeros((KS, BS), jnp.bfloat16)
    sd[null] = nul[...]


def sweep_kernel(count, blocks, added, distance, my_y, lists, tiles, mf, ms, md, sf, ss, sd, em, *refs):
    if added:
        before, out, rf, rs, rd, ids, owner = refs
    else:
        out, rf, rs, rd, ids, owner = refs
    target = (my_y[0] + distance) & (NY - 1)
    base = ((target & (NYL - 1)) * NYH + (target >> 1)) * NZ if added else 0
    null = count * SB
    slots = count * CAP // 2

    for j in range(blocks):
        q = split_pieces(tiles[base + j])
        for m, ref in ((mf, rf), (ms, rs), (md, rd)):
            ref[j] = lax.dot_general(
                q, m[...], (((0,), (1,)), ((), ())), preferred_element_type=jnp.float32
            ).astype(jnp.bfloat16)
        out[j] = before[base + j] if added else jnp.zeros((BS, BS), jnp.float32)

    def one_block(j, n):
        for t in range(slots):
            owner[n // 2 + t] = j
        for d in range(count):
            used = []
            for c in range(CAP):
                value = lists[d, (base + j) * CAP + c]
                ids[n + c] = d * SB + value
                used.append((value >= 0).astype(jnp.int32))
            n = n + ((used[0] + used[1]) + (used[2] + used[3]))
        ids[n] = null
        return n + n % 2

    n = lax.fori_loop(0, blocks, one_block, 0)
    for t in range(2 * UNROLL):
        ids[n + t] = null
    for t in range(UNROLL):
        owner[n // 2 + t] = 0

    def front(u):
        a, b = ids[2 * u], ids[2 * u + 1]
        j = owner[u]

        def pair(ref):
            return jnp.concatenate([ref[a], ref[b]], axis=1)

        facing = jnp.maximum(dot(rf[j], pair(sf)), 0.0)
        seen = jnp.maximum(dot(rs[j], pair(ss)), 0.0)
        spread = dot(rd[j], pair(sd))
        return (facing * seen / (spread * spread)).astype(jnp.bfloat16)

    def back(u, values):
        a, b = ids[2 * u], ids[2 * u + 1]
        j = owner[u]
        out[j] = out[j] + dot(values, jnp.concatenate([em[a], em[b]], axis=0))

    def step(i, carry):
        values = [front(i * UNROLL + r) for r in range(UNROLL)]
        for r in range(UNROLL):
            back(i * UNROLL + r, values[r])
        return carry

    lax.fori_loop(0, pl.cdiv(n // 2, UNROLL), step, 0)


VMEM_SPEC = pl.BlockSpec(memory_space=pltpu.VMEM)
SMEM_SPEC = pl.BlockSpec(memory_space=pltpu.SMEM)
BF16 = jnp.bfloat16
PARAMS = pltpu.CompilerParams(vmem_limit_bytes=VMEM_LIMIT)


def bf16_shape(*shape):
    return jax.ShapeDtypeStruct(shape, BF16)


def src_prep(me, packed, mats, nul):
    count = len(packed)
    rows = count * SB + 1
    return pl.pallas_call(
        functools.partial(src_prep_kernel, count),
        out_shape=[
            bf16_shape(rows, KF, BS),
            bf16_shape(rows, KS, BS),
            bf16_shape(rows, KD, BS),
            bf16_shape(rows, BS, BS),
            jax.ShapeDtypeStruct((count, BS), jnp.int32),
        ],
        in_specs=[SMEM_SPEC] + [VMEM_SPEC] * (count + 4),
        out_specs=[VMEM_SPEC] * 5,
        name="src_prep",
        compiler_params=PARAMS,
        cost_estimate=pl.CostEstimate(flops=10**6, bytes_accessed=10**6, transcendentals=0),
    )(me, *packed, *mats, nul)


def sweep(my_y, distance, tiles, mats, src, blocks, before=None):
    *src, lists = src
    count = lists.shape[0]
    extra = () if before is None else (before,)
    return pl.pallas_call(
        functools.partial(sweep_kernel, count, blocks, before is not None, distance),
        out_shape=jax.ShapeDtypeStruct((blocks, BS, BS), jnp.float32),
        in_specs=[SMEM_SPEC] * 2 + [VMEM_SPEC] * (8 + len(extra)),
        out_specs=VMEM_SPEC,
        scratch_shapes=[
            pltpu.VMEM((blocks, BS, KF), BF16),
            pltpu.VMEM((blocks, BS, KS), BF16),
            pltpu.VMEM((blocks, BS, KD), BF16),
            pltpu.SMEM((blocks * count * CAP + 4 * UNROLL,), jnp.int32),
            pltpu.SMEM((blocks * count * CAP // 2 + count * CAP + 2 * UNROLL,), jnp.int32),
        ],
        name="sweep",
        compiler_params=PARAMS,
        cost_estimate=pl.CostEstimate(flops=10**6, bytes_accessed=10**6, transcendentals=0),
    )(my_y, lists, tiles, *mats, *src, *extra)


def normals(angle_rows):
    polar = angle_rows[0]
    azimuth = angle_rows[1]
    return jnp.stack(
        [jnp.sin(polar) * jnp.cos(azimuth), jnp.sin(polar) * jnp.sin(azimuth), jnp.cos(polar)]
    )


def base_rows(pos, direction, extra):
    centred = pos - CENTRE
    coarse = jnp.round(centred * 32.0) * (1.0 / 32.0)
    fine = centred - coarse
    square_a = coarse[0] * coarse[0] + coarse[1] * coarse[1] + coarse[2] * coarse[2]
    square_b = (
        fine[0] * (2.0 * coarse[0] + fine[0])
        + fine[1] * (2.0 * coarse[1] + fine[1])
        + fine[2] * (2.0 * coarse[2] + fine[2])
    ) + extra
    along = -(
        direction[0] * centred[0] + direction[1] * centred[1] + direction[2] * centred[2]
    )
    rows = [centred, direction, along[None], square_a[None], square_b[None]]
    return jnp.concatenate(rows + [jnp.ones_like(along)[None]], axis=0)


def y_route(distance):
    def linear(y):
        return (y % NYL) * NYH + y // NYL

    return [(linear(y), linear((y + distance) % NY)) for y in range(NY)]


def shards(
    recv_pos,
    recv_angles,
    src_pos,
    src_angles,
    src_area,
    reemission,
    incident,
    direct,
    visible_lists,
    visible_counts,
):
    mats = selection_matrices()
    recv_mats = [jnp.asarray(r, BF16) for r, _ in mats]
    src_mats = [jnp.asarray(s, BF16) for _, s in mats]
    nul = jnp.asarray(null_spread(), BF16)

    scale = reemission * src_area * (1.0 / np.pi)
    rows = base_rows(src_pos, normals(src_angles) * scale, src_area)
    rows = rows.reshape(LST, SB, BS).transpose(1, 0, 2)
    slots = jnp.arange(CAP, dtype=jnp.int32)
    live = slots < visible_counts[0, 0][:, :, None]
    marked = jnp.where(live, visible_lists[0, 0], -1)
    marked = marked.reshape(NX, NYL, NC, NYH, NZ, CAP).transpose(0, 2, 1, 3, 4, 5)
    marked = marked.reshape(GROUP, 1, NJ * CAP).astype(jnp.float32)
    rest = jnp.zeros((SB, ROWS - LST - 1, BS), jnp.float32)
    tiles = jnp.concatenate([rows, marked, rest], axis=1).reshape(SB * ROWS, BS)
    mine = jnp.concatenate([incident.astype(jnp.float32), tiles], axis=0)

    def along_x(block, distance):
        return lax.ppermute(block, "x", [(i, (i + distance) % NX) for i in range(NX)])

    def other_core(block):
        return lax.ppermute(block, "c", [(0, 1), (1, 0)])

    me = (lax.axis_index("x") * NC + lax.axis_index("c")).astype(jnp.int32).reshape(1)
    my_y = (lax.axis_index("yh") * NYL + lax.axis_index("yl")).astype(jnp.int32).reshape(1)
    far = [along_x(mine, d) for d in (1, 3, 2)]
    near = [mine, other_core(mine)]

    recv_rows = base_rows(recv_pos, normals(recv_angles), jnp.zeros((BS,), jnp.float32))
    recv_tile = jnp.concatenate([recv_rows, jnp.zeros((ROWS - LST, BS), jnp.float32)], axis=0)
    tiles = lax.all_to_all(
        jnp.broadcast_to(recv_tile, (NJ, ROWS, BS)), ("yl", "yh", "z"), 0, 0, tiled=True
    )

    begun = sweep(my_y, 0, tiles, recv_mats, src_prep(me, near, src_mats, nul), NJ)
    far = lax.optimization_barrier((*far, begun))
    far, begun = list(far[:3]), far[3]
    far = far + [other_core(block) for block in far]
    src = src_prep(me, far, src_mats, nul)

    def chunk(distance):
        return sweep(my_y, distance, tiles, recv_mats, src, NZ, begun)

    def along_y(block, distance):
        return lax.ppermute(block, ("yl", "yh"), y_route(distance))

    arrived = [along_y(chunk(d), d) for d in (2, 1, 3)]
    total = chunk(0) + arrived[0] + arrived[1] + arrived[2]
    pieces = lax.all_to_all(total, "z", 0, 0, tiled=True)
    return direct + jnp.sum(pieces, axis=0)


def solution(mesh):
    fine = Mesh(mesh.devices.reshape(NX, NYL, NC, NYH, NZ), ("x", "yl", "c", "yh", "z"))
    blk, lane = ("x", "yl", "c"), ("yh", "z")
    both = blk + lane
    return jax.shard_map(
        shards,
        mesh=fine,
        in_specs=(
            P(None, both),
            P(None, both),
            P(None, both),
            P(None, both),
            P(both),
            P(both),
            P(both, None),
            P(both, None),
            P(blk, lane, None, None, None),
            P(blk, lane, None, None),
        ),
        out_specs=P(both, None),
        check_vma=False,
    )
```

```python
import functools

import jax
import jax.numpy as jnp
import numpy as np
from jax import lax
from jax.experimental import pallas as pl
from jax.experimental.pallas import tpu as pltpu
from jax.sharding import Mesh
from jax.sharding import PartitionSpec as P

NX, NYL, NC, NYH, NZ = 4, 2, 2, 2, 8
NY = NYL * NYH
BS = 128
SB = 8
CAP = 4
GROUP = NX * NC
NJ = NY * NZ
CENTRE = 3.0
TILE = 16
POS, NRM, AREA = 0, 3, 6
ROWS, DOT, SQA, SQB, ONE = 16, 8, 9, 10, 11
KF, KS, KD = 32, 32, 48
VMEM_LIMIT = 16 << 20
UNROLL = 8


def selection_matrices():
    pieces = [(i, j) for i in range(3) for j in range(3) if i + j < 4]

    def build(depth, terms):
        recv = np.zeros((depth, 3 * ROWS), np.float32)
        src = np.zeros((depth, 3 * ROWS), np.float32)
        for at, (scale, ri, rrow, si, srow) in enumerate(terms):
            recv[at, ri * ROWS + rrow] = scale
            src[at, si * ROWS + srow] = 1.0
        return recv, src

    def product(scale, rrow, srow):
        return [(scale, i, rrow + a, j, srow + a) for i, j in pieces for a in range(3)]

    def from_recv(row, count):
        return [(1.0, i, row, 0, ONE) for i in range(count)]

    def from_src(row, count):
        return [(1.0, 0, ONE, i, row) for i in range(count)]

    facing = product(1.0, NRM, POS) + from_recv(DOT, 3)
    seen = product(1.0, POS, NRM) + from_src(DOT, 3)
    cross = product(-2.0, POS, POS)
    spread = (
        from_recv(SQA, 2) + from_src(SQA, 2) + cross + from_recv(SQB, 3) + from_src(SQB, 3)
    )
    return [build(KF, facing), build(KS, seen), build(KD, spread)]


def null_spread():
    column = np.zeros((KD, BS), np.float32)
    column[2, :] = 1.0
    return column


def split_pieces(tile):
    row = lax.broadcasted_iota(jnp.int32, tile.shape, 0)
    fixed = row < NRM
    coarse = jnp.where(fixed, jnp.round(tile * 32.0) * (1.0 / 32.0), tile)
    along = -(
        tile[NRM : NRM + 1] * tile[POS : POS + 1]
        + tile[NRM + 1 : NRM + 2] * tile[POS + 1 : POS + 2]
        + tile[NRM + 2 : NRM + 3] * tile[POS + 2 : POS + 3]
    )
    grid = [coarse[a : a + 1] for a in range(3)]
    fine = [tile[a : a + 1] - grid[a] for a in range(3)]
    square_a = grid[0] * grid[0] + grid[1] * grid[1] + grid[2] * grid[2]
    square_b = (
        fine[0] * (2.0 * grid[0] + fine[0])
        + fine[1] * (2.0 * grid[1] + fine[1])
        + fine[2] * (2.0 * grid[2] + fine[2])
    ) + tile[AREA : AREA + 1]
    derived = jnp.where(
        row == 0,
        along,
        jnp.where(
            row == 1, square_a, jnp.where(row == 2, square_b, jnp.where(row == 3, 1.0, 0.0))
        ),
    )
    values = jnp.concatenate([tile, derived], axis=0)
    high = jnp.concatenate([coarse, derived], axis=0).astype(jnp.bfloat16)
    rest = values - high.astype(jnp.float32)
    cut = lax.broadcasted_iota(jnp.int32, values.shape, 0) < NRM
    mid = jnp.where(cut, jnp.round(rest * 8192.0) * (1.0 / 8192.0), rest).astype(jnp.bfloat16)
    low = (rest - mid.astype(jnp.float32)).astype(jnp.bfloat16)
    return jnp.concatenate([high, mid, low], axis=0)


def dot(a, b):
    return jnp.dot(a, b, preferred_element_type=jnp.float32)


def direction(angles):
    polar, azimuth = angles[0:1], angles[1:2]
    across = jnp.sin(polar)
    return [across * jnp.cos(azimuth), across * jnp.sin(azimuth), jnp.cos(polar)]


def pack_kernel(
    incident, pos, angles, area, keep, lists, counts, recv_pos, recv_angles, packed, recv_tile
):
    packed[: SB * BS, :] = incident[...].astype(jnp.float32)
    packed[SB * BS :, :] = jnp.zeros((SB * TILE, BS), jnp.float32)
    scale = keep[...] * area[...] * (1.0 / np.pi)
    rows = [pos[a : a + 1, :] - CENTRE for a in range(3)]
    rows += [component * scale for component in direction(angles[...])]
    rows += [area[...], jnp.zeros_like(scale)]
    tile = jnp.concatenate(rows, axis=0)
    slot = lax.broadcasted_iota(jnp.int32, (CAP, NYH * NZ), 0)
    for k in range(SB):
        at = SB * BS + k * TILE
        packed[at : at + 8, :] = tile[:, k * BS : (k + 1) * BS]
        for yl in range(NYL):
            slab = ((k // NC) * NYL + yl) * NC + k % NC
            live = slot < counts[slab : slab + 1, :]
            marked = jnp.where(live, lists[slab], -1).astype(jnp.float32)
            packed[at + 8 + yl * CAP : at + 8 + (yl + 1) * CAP, : NYH * NZ] = marked
    rows = [recv_pos[a : a + 1, :] - CENTRE for a in range(3)]
    rows += direction(recv_angles[...])
    rows += [jnp.zeros((2, BS), jnp.float32)]
    tile = jnp.concatenate(rows, axis=0)
    for j in range(NJ):
        recv_tile[j] = tile


def src_prep_kernel(count, me, *refs):
    packed = refs[:count]
    mf, ms, md, nul, sf, ss, sd, em, lists = refs[count:]
    list_at = SB * BS + me[0] * TILE + 8
    for d in range(count):
        ref = packed[d]
        for k in range(SB):
            em[d * SB + k] = ref[k * BS : (k + 1) * BS, :].astype(jnp.bfloat16)
        tiles = [ref[SB * BS + k * TILE : SB * BS + k * TILE + 8, :] for k in range(SB)]
        q = split_pieces(jnp.concatenate(tiles, axis=1))
        lists[d] = ref[pl.ds(pl.multiple_of(list_at, 8), 8), :].astype(jnp.int32)
        for m, out in ((mf, sf), (ms, ss), (md, sd)):
            values = dot(m[...], q).astype(jnp.bfloat16)
            for k in range(SB):
                out[d * SB + k] = values[:, k * BS : (k + 1) * BS]
    null = count * SB
    em[null] = jnp.zeros((BS, BS), jnp.bfloat16)
    sf[null] = jnp.zeros((KF, BS), jnp.bfloat16)
    ss[null] = jnp.zeros((KS, BS), jnp.bfloat16)
    sd[null] = nul[...]


def sweep_kernel(count, blocks, added, distance, my_y, lists, tiles, mf, ms, md, sf, ss, sd, em, *refs):
    if added:
        before, out, rf, rs, rd, ids, owner = refs
    else:
        out, rf, rs, rd, ids, owner = refs
    target = (my_y[0] + distance) & (NY - 1)
    base = ((target & (NYL - 1)) * NYH + (target >> 1)) * NZ if added else 0
    null = count * SB
    slots = count * CAP // 2

    for j in range(blocks):
        q = split_pieces(tiles[base + j])
        for m, ref in ((mf, rf), (ms, rs), (md, rd)):
            ref[j] = lax.dot_general(
                q, m[...], (((0,), (1,)), ((), ())), preferred_element_type=jnp.float32
            ).astype(jnp.bfloat16)
        out[j] = before[base + j] if added else jnp.zeros((BS, BS), jnp.float32)

    def one_block(j, n):
        row = (((base + j) >> 4)) * CAP
        lane = (base + j) & (NYH * NZ - 1)
        for t in range(slots):
            owner[n // 2 + t] = j
        for d in range(count):
            used = []
            for c in range(CAP):
                value = lists[d, row + c, lane]
                ids[n + c] = d * SB + value
                used.append((value >= 0).astype(jnp.int32))
            n = n + ((used[0] + used[1]) + (used[2] + used[3]))
        ids[n] = null
        return n + n % 2

    n = lax.fori_loop(0, blocks, one_block, 0)
    for t in range(2 * UNROLL):
        ids[n + t] = null
    for t in range(UNROLL):
        owner[n // 2 + t] = 0

    def front(u):
        a, b = ids[2 * u], ids[2 * u + 1]
        j = owner[u]

        def pair(ref):
            return jnp.concatenate([ref[a], ref[b]], axis=1)

        facing = jnp.maximum(dot(rf[j], pair(sf)), 0.0)
        seen = jnp.maximum(dot(rs[j], pair(ss)), 0.0)
        spread = dot(rd[j], pair(sd))
        return (facing * seen / (spread * spread)).astype(jnp.bfloat16)

    def back(u, values):
        a, b = ids[2 * u], ids[2 * u + 1]
        j = owner[u]
        out[j] = out[j] + dot(values, jnp.concatenate([em[a], em[b]], axis=0))

    def step(i, carry):
        values = [front(i * UNROLL + r) for r in range(UNROLL)]
        for r in range(UNROLL):
            back(i * UNROLL + r, values[r])
        return carry

    lax.fori_loop(0, pl.cdiv(n // 2, UNROLL), step, 0)


VMEM_SPEC = pl.BlockSpec(memory_space=pltpu.VMEM)
SMEM_SPEC = pl.BlockSpec(memory_space=pltpu.SMEM)
BF16 = jnp.bfloat16
PARAMS = pltpu.CompilerParams(vmem_limit_bytes=VMEM_LIMIT)


def bf16_shape(*shape):
    return jax.ShapeDtypeStruct(shape, BF16)


def src_prep(me, packed, mats, nul):
    count = len(packed)
    rows = count * SB + 1
    return pl.pallas_call(
        functools.partial(src_prep_kernel, count),
        out_shape=[
            bf16_shape(rows, KF, BS),
            bf16_shape(rows, KS, BS),
            bf16_shape(rows, KD, BS),
            bf16_shape(rows, BS, BS),
            jax.ShapeDtypeStruct((count, 8, BS), jnp.int32),
        ],
        in_specs=[SMEM_SPEC] + [VMEM_SPEC] * (count + 4),
        out_specs=[VMEM_SPEC] * 5,
        name="src_prep",
        compiler_params=PARAMS,
        cost_estimate=pl.CostEstimate(flops=10**6, bytes_accessed=10**6, transcendentals=0),
    )(me, *packed, *mats, nul)


def sweep(my_y, distance, tiles, mats, src, blocks, before=None):
    *src, lists = src
    count = lists.shape[0]
    extra = () if before is None else (before,)
    return pl.pallas_call(
        functools.partial(sweep_kernel, count, blocks, before is not None, distance),
        out_shape=jax.ShapeDtypeStruct((blocks, BS, BS), jnp.float32),
        in_specs=[SMEM_SPEC] * 2 + [VMEM_SPEC] * (8 + len(extra)),
        out_specs=VMEM_SPEC,
        scratch_shapes=[
            pltpu.VMEM((blocks, BS, KF), BF16),
            pltpu.VMEM((blocks, BS, KS), BF16),
            pltpu.VMEM((blocks, BS, KD), BF16),
            pltpu.SMEM((blocks * count * CAP + 4 * UNROLL,), jnp.int32),
            pltpu.SMEM((blocks * count * CAP // 2 + count * CAP + 2 * UNROLL,), jnp.int32),
        ],
        name="sweep",
        compiler_params=PARAMS,
        cost_estimate=pl.CostEstimate(flops=10**6, bytes_accessed=10**6, transcendentals=0),
    )(my_y, lists, tiles, *mats, *src, *extra)


def pack(*operands):
    return pl.pallas_call(
        pack_kernel,
        out_shape=[
            jax.ShapeDtypeStruct((SB * (BS + TILE), BS), jnp.float32),
            jax.ShapeDtypeStruct((NJ, 8, BS), jnp.float32),
        ],
        in_specs=[VMEM_SPEC] * 9,
        out_specs=[VMEM_SPEC] * 2,
        name="pack",
        compiler_params=PARAMS,
        cost_estimate=pl.CostEstimate(flops=10**6, bytes_accessed=10**6, transcendentals=0),
    )(*operands)


def y_route(distance):
    def linear(y):
        return (y % NYL) * NYH + y // NYL

    return [(linear(y), linear((y + distance) % NY)) for y in range(NY)]


def shards(
    recv_pos,
    recv_angles,
    src_pos,
    src_angles,
    src_area,
    reemission,
    incident,
    direct,
    visible_lists,
    visible_counts,
):
    mats = selection_matrices()
    recv_mats = [jnp.asarray(r, BF16) for r, _ in mats]
    src_mats = [jnp.asarray(s, BF16) for _, s in mats]
    nul = jnp.asarray(null_spread(), BF16)

    mine, recv_tile = pack(
        incident,
        src_pos,
        src_angles,
        src_area.reshape(1, SB * BS),
        reemission.reshape(1, SB * BS),
        visible_lists[0, 0].transpose(0, 2, 1),
        visible_counts[0, 0],
        recv_pos,
        recv_angles,
    )

    def along_x(block, distance):
        return lax.ppermute(block, "x", [(i, (i + distance) % NX) for i in range(NX)])

    def other_core(block):
        return lax.ppermute(block, "c", [(0, 1), (1, 0)])

    me = (lax.axis_index("x") * NC + lax.axis_index("c")).astype(jnp.int32).reshape(1)
    my_y = (lax.axis_index("yh") * NYL + lax.axis_index("yl")).astype(jnp.int32).reshape(1)
    far = [along_x(mine, d) for d in (1, 3, 2)]
    near = [mine, other_core(mine)]

    tiles = lax.all_to_all(recv_tile, ("yl", "yh", "z"), 0, 0, tiled=True)

    near = src_prep(me, near, src_mats, nul)
    begun = sweep(my_y, 0, tiles, recv_mats, near, NJ)
    far = lax.optimization_barrier((*far, tiles, near[0]))
    far = list(far[:3])
    far = far + [other_core(block) for block in far]
    src = src_prep(me, far, src_mats, nul)

    def chunk(distance):
        return sweep(my_y, distance, tiles, recv_mats, src, NZ, begun)

    def along_y(block, distance):
        return lax.ppermute(block, ("yl", "yh"), y_route(distance))

    arrived = [along_y(chunk(d), d) for d in (2, 1, 3)]
    total = chunk(0) + arrived[0] + arrived[1] + arrived[2]
    pieces = lax.all_to_all(total, "z", 0, 0, tiled=True)
    return direct + jnp.sum(pieces, axis=0)


def solution(mesh):
    fine = Mesh(mesh.devices.reshape(NX, NYL, NC, NYH, NZ), ("x", "yl", "c", "yh", "z"))
    blk, lane = ("x", "yl", "c"), ("yh", "z")
    both = blk + lane
    return jax.shard_map(
        shards,
        mesh=fine,
        in_specs=(
            P(None, both),
            P(None, both),
            P(None, both),
            P(None, both),
            P(both),
            P(both),
            P(both, None),
            P(both, None),
            P(blk, lane, None, None, None),
            P(blk, lane, None, None),
        ),
        out_specs=P(both, None),
        check_vma=False,
    )
```

```python
import functools

import jax
import jax.numpy as jnp
import numpy as np
from jax import lax
from jax.experimental import pallas as pl
from jax.experimental.pallas import tpu as pltpu
from jax.sharding import Mesh
from jax.sharding import PartitionSpec as P

NX, NYL, NC, NYH, NZ = 4, 2, 2, 2, 8
NY = NYL * NYH
BS = 128
SB = 8
CAP = 4
GROUP = NX * NC
NJ = NY * NZ
CENTRE = 3.0
TILE = 16
POS, NRM, AREA = 0, 3, 6
ROWS, DOT, SQA, SQB, ONE = 16, 8, 9, 10, 11
KF, KS, KD = 32, 32, 48
VMEM_LIMIT = 16 << 20
UNROLL, TAIL = 16, 4
HALF = NZ // 2
FIRST = 4 * BS


def contraction_terms():
    pieces = [(i, j) for i in range(3) for j in range(3) if i + j < 4]

    def product(scale, rrow, srow):
        return [
            (scale, i * ROWS + rrow + a, j * ROWS + srow + a) for i, j in pieces for a in range(3)
        ]

    def from_recv(row, count):
        return [(1.0, i * ROWS + row, ONE) for i in range(count)]

    def from_src(row, count):
        return [(1.0, ONE, i * ROWS + row) for i in range(count)]

    facing = product(1.0, NRM, POS) + from_recv(DOT, 3)
    seen = product(1.0, POS, NRM) + from_src(DOT, 3)
    cross = product(-2.0, POS, POS)
    spread = (
        from_src(SQA, 2) + from_recv(SQA, 2) + cross + from_recv(SQB, 3) + from_src(SQB, 3)
    )
    return (KF, facing), (KS, seen), (KD, spread)


def selections(side):
    made = []
    for depth, terms in contraction_terms():
        groups = []
        for start in range(0, depth, 8):
            row = lax.broadcasted_iota(jnp.int32, (8, 3 * ROWS), 0)
            column = lax.broadcasted_iota(jnp.int32, (8, 3 * ROWS), 1)
            group = jnp.zeros((8, 3 * ROWS), jnp.float32)
            for at, term in enumerate(terms[start : start + 8]):
                value = term[0] if side == 0 else 1.0
                here = (row == at) & (column == term[1 + side])
                group = jnp.where(here, value, group)
            groups.append(group)
        made.append(jnp.concatenate(groups, axis=0).astype(jnp.bfloat16))
    return made


def split_pieces(tile):
    row = lax.broadcasted_iota(jnp.int32, tile.shape, 0)
    fixed = row < NRM
    coarse = jnp.where(fixed, jnp.round(tile * 32.0) * (1.0 / 32.0), tile)
    along = -(
        tile[NRM : NRM + 1] * tile[POS : POS + 1]
        + tile[NRM + 1 : NRM + 2] * tile[POS + 1 : POS + 2]
        + tile[NRM + 2 : NRM + 3] * tile[POS + 2 : POS + 3]
    )
    grid = [coarse[a : a + 1] for a in range(3)]
    fine = [tile[a : a + 1] - grid[a] for a in range(3)]
    square_a = grid[0] * grid[0] + grid[1] * grid[1] + grid[2] * grid[2]
    square_b = (
        fine[0] * (2.0 * grid[0] + fine[0])
        + fine[1] * (2.0 * grid[1] + fine[1])
        + fine[2] * (2.0 * grid[2] + fine[2])
    ) + tile[AREA : AREA + 1]
    derived = jnp.where(
        row == 0,
        along,
        jnp.where(
            row == 1, square_a, jnp.where(row == 2, square_b, jnp.where(row == 3, 1.0, 0.0))
        ),
    )
    values = jnp.concatenate([tile, derived], axis=0)
    high = jnp.concatenate([coarse, derived], axis=0).astype(jnp.bfloat16)
    rest = values - high.astype(jnp.float32)
    cut = lax.broadcasted_iota(jnp.int32, values.shape, 0) < NRM
    mid = jnp.where(cut, jnp.round(rest * 8192.0) * (1.0 / 8192.0), rest).astype(jnp.bfloat16)
    low = (rest - mid.astype(jnp.float32)).astype(jnp.bfloat16)
    return jnp.concatenate([high, mid, low], axis=0)


def dot(a, b):
    return jnp.dot(a, b, preferred_element_type=jnp.float32)


def direction(angles):
    polar, azimuth = angles[0:1], angles[1:2]
    across = jnp.sin(polar)
    return [across * jnp.cos(azimuth), across * jnp.sin(azimuth), jnp.cos(polar)]


def pack_kernel(
    incident, pos, angles, area, keep, lists, counts, recv_pos, recv_angles, packed, recv_tile
):
    packed[: SB * BS, :] = incident[...].astype(jnp.float32)
    packed[SB * BS :, :] = jnp.zeros((SB * TILE, BS), jnp.float32)
    scale = keep[...] * area[...] * (1.0 / np.pi)
    rows = [pos[a : a + 1, :] - CENTRE for a in range(3)]
    rows += [component * scale for component in direction(angles[...])]
    rows += [area[...], jnp.zeros_like(scale)]
    tile = jnp.concatenate(rows, axis=0)
    slot = lax.broadcasted_iota(jnp.int32, (CAP, NYH * NZ), 0)
    for k in range(SB):
        at = SB * BS + k * TILE
        packed[at : at + 8, :] = tile[:, k * BS : (k + 1) * BS]
        for yl in range(NYL):
            slab = ((k // NC) * NYL + yl) * NC + k % NC
            live = slot < counts[slab : slab + 1, :]
            marked = jnp.where(live, lists[slab], -1).astype(jnp.float32)
            packed[at + 8 + yl * CAP : at + 8 + (yl + 1) * CAP, : NYH * NZ] = marked
    rows = [recv_pos[a : a + 1, :] - CENTRE for a in range(3)]
    rows += direction(recv_angles[...])
    rows += [jnp.zeros((2, BS), jnp.float32)]
    tile = jnp.concatenate(rows, axis=0)
    for j in range(NJ):
        recv_tile[j] = tile


def src_prep_kernel(count, cut, me, *refs):
    inputs = count + cut
    sf, ss, sd, em, lists = refs[inputs:]
    mats = selections(1)

    def rows_of(d):
        if d < count - cut:
            return lambda start, size: refs[d][pl.ds(start, size), :]
        first, second = refs[count - cut + 2 * (d - count + cut) :][:2]

        def rows(start, size):
            if isinstance(start, int) and start < FIRST:
                return first[pl.ds(start, size), :]
            return second[pl.ds(start - FIRST, size), :]

        return rows

    for d in range(count):
        rows = rows_of(d)
        for k in range(SB):
            em[d * SB + k] = rows(k * BS, BS).astype(jnp.bfloat16)
        tiles = [rows(SB * BS + k * TILE, 8) for k in range(SB)]
        q = split_pieces(jnp.concatenate(tiles, axis=1))
        list_at = pl.multiple_of(SB * BS + me[0] * TILE + 8, 8)
        lists[d] = rows(list_at, 8).astype(jnp.int32)
        for m, out in zip(mats, (sf, ss, sd)):
            values = dot(m, q).astype(jnp.bfloat16)
            for k in range(SB):
                out[d * SB + k] = values[:, k * BS : (k + 1) * BS]
    null = count * SB
    em[null] = jnp.zeros((BS, BS), jnp.bfloat16)
    sf[null] = jnp.zeros((KF, BS), jnp.bfloat16)
    ss[null] = jnp.zeros((KS, BS), jnp.bfloat16)
    first_row = lax.broadcasted_iota(jnp.int32, (KD, BS), 0) == 0
    sd[null] = jnp.where(first_row, 1.0, 0.0).astype(jnp.bfloat16)


def sweep_kernel(count, blocks, added, distance, my_y, lists, tiles, sf, ss, sd, em, *refs):
    if added == 2:
        before, passing, out, rf, rs, rd, ids, owner = refs
    elif added:
        before, out, rf, rs, rd, ids, owner = refs
    else:
        out, rf, rs, rd, ids, owner = refs
    target = (my_y[0] + distance) & (NY - 1)
    base = ((target & (NYL - 1)) * NYH + (target >> 1)) * NZ if blocks == NZ else 0
    null = count * SB
    slots = count * CAP // 2

    mats = selections(0)
    for j in range(blocks):
        q = split_pieces(tiles[base + j])
        for m, ref in zip(mats, (rf, rs, rd)):
            ref[j] = lax.dot_general(
                q, m, (((0,), (1,)), ((), ())), preferred_element_type=jnp.float32
            ).astype(jnp.bfloat16)
        start = before[base + j] if added else jnp.zeros((BS, BS), jnp.float32)
        out[j] = start + passing[j - HALF] if added == 2 and j >= HALF else start

    def one_block(j, n):
        row = (((base + j) >> 4)) * CAP
        lane = (base + j) & (NYH * NZ - 1)
        for t in range(slots):
            owner[n // 2 + t] = j
        for d in range(count):
            used = []
            for c in range(CAP):
                value = lists[d, row + c, lane]
                ids[n + c] = d * SB + value
                used.append((value >= 0).astype(jnp.int32))
            n = n + ((used[0] + used[1]) + (used[2] + used[3]))
        ids[n] = null
        return n + n % 2

    n = lax.fori_loop(0, blocks, one_block, 0)
    for t in range(2 * TAIL):
        ids[n + t] = null
    for t in range(TAIL):
        owner[n // 2 + t] = 0

    def front(u):
        a, b = ids[2 * u], ids[2 * u + 1]
        j = owner[u]

        def pair(ref):
            return jnp.concatenate([ref[a], ref[b]], axis=1)

        facing = jnp.maximum(dot(rf[j], pair(sf)), 0.0)
        seen = jnp.maximum(dot(rs[j], pair(ss)), 0.0)
        spread = dot(rd[j], pair(sd))
        return (facing * seen / (spread * spread)).astype(jnp.bfloat16)

    def back(u, values):
        a, b = ids[2 * u], ids[2 * u + 1]
        j = owner[u]
        out[j] = out[j] + dot(values, jnp.concatenate([em[a], em[b]], axis=0))

    def run(first_unit, width, steps):
        def step(i, carry):
            units = [first_unit + i * width + r for r in range(width)]
            values = [front(u) for u in units]
            for u, value in zip(units, values):
                back(u, value)
            return carry

        lax.fori_loop(0, steps, step, 0)

    units = n // 2
    long = units // UNROLL
    run(0, UNROLL, long)
    run(long * UNROLL, TAIL, pl.cdiv(units - long * UNROLL, TAIL))


VMEM_SPEC = pl.BlockSpec(memory_space=pltpu.VMEM)
SMEM_SPEC = pl.BlockSpec(memory_space=pltpu.SMEM)
BF16 = jnp.bfloat16
PARAMS = pltpu.CompilerParams(vmem_limit_bytes=VMEM_LIMIT)


def bf16_shape(*shape):
    return jax.ShapeDtypeStruct(shape, BF16)


def src_prep(me, whole, parts=()):
    packed = whole + [part for pair in parts for part in pair]
    count = len(whole) + len(parts)
    rows = count * SB + 1
    return pl.pallas_call(
        functools.partial(src_prep_kernel, count, len(parts)),
        out_shape=[
            bf16_shape(rows, KF, BS),
            bf16_shape(rows, KS, BS),
            bf16_shape(rows, KD, BS),
            bf16_shape(rows, BS, BS),
            jax.ShapeDtypeStruct((count, 8, BS), jnp.int32),
        ],
        in_specs=[SMEM_SPEC] + [VMEM_SPEC] * len(packed),
        out_specs=[VMEM_SPEC] * 5,
        name="src_prep",
        compiler_params=PARAMS,
        cost_estimate=pl.CostEstimate(flops=10**6, bytes_accessed=10**6, transcendentals=0),
    )(me, *packed)


def sweep(my_y, distance, tiles, src, blocks, *extra):
    *src, lists = src
    count = lists.shape[0]
    return pl.pallas_call(
        functools.partial(sweep_kernel, count, blocks, len(extra), distance),
        out_shape=jax.ShapeDtypeStruct((blocks, BS, BS), jnp.float32),
        in_specs=[SMEM_SPEC] * 2 + [VMEM_SPEC] * (5 + len(extra)),
        out_specs=VMEM_SPEC,
        scratch_shapes=[
            pltpu.VMEM((blocks, BS, KF), BF16),
            pltpu.VMEM((blocks, BS, KS), BF16),
            pltpu.VMEM((blocks, BS, KD), BF16),
            pltpu.SMEM((blocks * count * CAP + 4 * UNROLL,), jnp.int32),
            pltpu.SMEM((blocks * count * CAP // 2 + count * CAP + 2 * UNROLL,), jnp.int32),
        ],
        name="sweep",
        compiler_params=PARAMS,
        cost_estimate=pl.CostEstimate(flops=10**6, bytes_accessed=10**6, transcendentals=0),
    )(my_y, lists, tiles, *src, *extra)


def pack(*operands):
    return pl.pallas_call(
        pack_kernel,
        out_shape=[
            jax.ShapeDtypeStruct((SB * (BS + TILE), BS), jnp.float32),
            jax.ShapeDtypeStruct((NJ, 8, BS), jnp.float32),
        ],
        in_specs=[VMEM_SPEC] * 9,
        out_specs=[VMEM_SPEC] * 2,
        name="pack",
        compiler_params=pltpu.CompilerParams(vmem_limit_bytes=60 << 20),
        cost_estimate=pl.CostEstimate(flops=10**6, bytes_accessed=10**6, transcendentals=0),
    )(*operands)


def y_route(distance):
    def linear(y):
        return (y % NYL) * NYH + y // NYL

    return [(linear(y), linear((y + distance) % NY)) for y in range(NY)]


def shards(
    recv_pos,
    recv_angles,
    src_pos,
    src_angles,
    src_area,
    reemission,
    incident,
    direct,
    visible_lists,
    visible_counts,
):
    mine, recv_tile = pack(
        incident,
        src_pos,
        src_angles,
        src_area.reshape(1, SB * BS),
        reemission.reshape(1, SB * BS),
        visible_lists[0, 0].transpose(0, 2, 1),
        visible_counts[0, 0],
        recv_pos,
        recv_angles,
    )

    def along_x(block, distance):
        return lax.ppermute(block, "x", [(i, (i + distance) % NX) for i in range(NX)])

    def other_core(block):
        return lax.ppermute(block, "c", [(0, 1), (1, 0)])

    me = (lax.axis_index("x") * NC + lax.axis_index("c")).astype(jnp.int32).reshape(1)
    my_y = (lax.axis_index("yh") * NYL + lax.axis_index("yl")).astype(jnp.int32).reshape(1)
    left, right = along_x(mine, 1), along_x(mine, 3)
    own = other_core(mine)

    tiles = lax.all_to_all(recv_tile, ("yl", "yh", "z"), 0, 0, tiled=True)

    near = src_prep(me, [mine, own])
    left, right, tiles, first = lax.optimization_barrier((left, right, tiles, near[0]))
    near = [first, *near[1:]]
    far = [along_x(left[:FIRST], 1), along_x(right[FIRST:], 3)]
    sides = [left, right, other_core(left), other_core(right)]

    begun = sweep(my_y, 0, tiles, near, NJ)
    *far, begun = lax.optimization_barrier((*far, begun))
    src = src_prep(me, sides, [far, [other_core(part) for part in far]])

    def along_y(block, distance):
        return lax.ppermute(block, ("yl", "yh"), y_route(distance))

    def part(distance, *passing):
        return sweep(my_y, distance, tiles, src, NZ, begun, *passing)

    across = part(2)
    by_left, by_right = along_y(across[:HALF], 1), along_y(across[HALF:], 3)
    ahead = part(1)
    ahead = along_y(jnp.concatenate([ahead[:HALF] + by_left, ahead[HALF:]], axis=0), 1)
    behind = along_y(part(3, by_right), 3)
    total = part(0) + ahead + behind
    pieces = lax.all_to_all(total, "z", 0, 0, tiled=True)
    return direct + jnp.sum(pieces, axis=0)


def solution(mesh):
    fine = Mesh(mesh.devices.reshape(NX, NYL, NC, NYH, NZ), ("x", "yl", "c", "yh", "z"))
    blk, lane = ("x", "yl", "c"), ("yh", "z")
    both = blk + lane
    return jax.shard_map(
        shards,
        mesh=fine,
        in_specs=(
            P(None, both),
            P(None, both),
            P(None, both),
            P(None, both),
            P(both),
            P(both),
            P(both, None),
            P(both, None),
            P(blk, lane, None, None, None),
            P(blk, lane, None, None),
        ),
        out_specs=P(both, None),
        check_vma=False,
    )
```

```python
import functools

import jax
import jax.numpy as jnp
import numpy as np
from jax import lax
from jax.experimental import pallas as pl
from jax.experimental.pallas import tpu as pltpu
from jax.sharding import Mesh
from jax.sharding import PartitionSpec as P

NX, NYL, NC, NYH, NZ = 4, 2, 2, 2, 8
NY = NYL * NYH
BS = 128
SB = 8
CAP = 4
GROUP = NX * NC
NJ = NY * NZ
CENTRE = 3.0
TILE = 16
POS, NRM, AREA = 0, 3, 6
ROWS, DOT, SQA, SQB, ONE = 16, 8, 9, 10, 11
KF, KS, KD = 32, 32, 48
VMEM_LIMIT = 16 << 20
UNROLL, TAIL = 16, 8
HALF = NZ // 2
FIRST = 4 * BS


def contraction_terms():
    pieces = [(i, j) for i in range(3) for j in range(3) if i + j < 4]

    def product(scale, rrow, srow):
        return [
            (scale, i * ROWS + rrow + a, j * ROWS + srow + a) for i, j in pieces for a in range(3)
        ]

    def from_recv(row, count):
        return [(1.0, i * ROWS + row, ONE) for i in range(count)]

    def from_src(row, count):
        return [(1.0, ONE, i * ROWS + row) for i in range(count)]

    facing = product(1.0, NRM, POS) + from_recv(DOT, 3)
    seen = product(1.0, POS, NRM) + from_src(DOT, 3)
    cross = product(-2.0, POS, POS)
    spread = (
        from_src(SQA, 2) + from_recv(SQA, 2) + cross + from_recv(SQB, 3) + from_src(SQB, 3)
    )
    return (KF, facing), (KS, seen), (KD, spread)


def selections(side):
    made = []
    for depth, terms in contraction_terms():
        groups = []
        for start in range(0, depth, 8):
            row = lax.broadcasted_iota(jnp.int32, (8, 3 * ROWS), 0)
            column = lax.broadcasted_iota(jnp.int32, (8, 3 * ROWS), 1)
            group = jnp.zeros((8, 3 * ROWS), jnp.float32)
            for at, term in enumerate(terms[start : start + 8]):
                value = term[0] if side == 0 else 1.0
                here = (row == at) & (column == term[1 + side])
                group = jnp.where(here, value, group)
            groups.append(group)
        made.append(jnp.concatenate(groups, axis=0).astype(jnp.bfloat16))
    return made


def split_pieces(tile):
    row = lax.broadcasted_iota(jnp.int32, tile.shape, 0)
    fixed = row < NRM
    coarse = jnp.where(fixed, jnp.round(tile * 32.0) * (1.0 / 32.0), tile)
    along = -(
        tile[NRM : NRM + 1] * tile[POS : POS + 1]
        + tile[NRM + 1 : NRM + 2] * tile[POS + 1 : POS + 2]
        + tile[NRM + 2 : NRM + 3] * tile[POS + 2 : POS + 3]
    )
    grid = [coarse[a : a + 1] for a in range(3)]
    fine = [tile[a : a + 1] - grid[a] for a in range(3)]
    square_a = grid[0] * grid[0] + grid[1] * grid[1] + grid[2] * grid[2]
    square_b = (
        fine[0] * (2.0 * grid[0] + fine[0])
        + fine[1] * (2.0 * grid[1] + fine[1])
        + fine[2] * (2.0 * grid[2] + fine[2])
    ) + tile[AREA : AREA + 1]
    derived = jnp.where(
        row == 0,
        along,
        jnp.where(
            row == 1, square_a, jnp.where(row == 2, square_b, jnp.where(row == 3, 1.0, 0.0))
        ),
    )
    values = jnp.concatenate([tile, derived], axis=0)
    high = jnp.concatenate([coarse, derived], axis=0).astype(jnp.bfloat16)
    rest = values - high.astype(jnp.float32)
    cut = lax.broadcasted_iota(jnp.int32, values.shape, 0) < NRM
    mid = jnp.where(cut, jnp.round(rest * 8192.0) * (1.0 / 8192.0), rest).astype(jnp.bfloat16)
    low = (rest - mid.astype(jnp.float32)).astype(jnp.bfloat16)
    return jnp.concatenate([high, mid, low], axis=0)


def dot(a, b):
    return jnp.dot(a, b, preferred_element_type=jnp.float32)


def direction(angles):
    polar, azimuth = angles[0:1], angles[1:2]
    across = jnp.sin(polar)
    return [across * jnp.cos(azimuth), across * jnp.sin(azimuth), jnp.cos(polar)]


def pack_kernel(
    incident, pos, angles, area, keep, lists, counts, recv_pos, recv_angles, first, second, recv_tile
):
    first[...] = incident[:FIRST, :].astype(jnp.float32)
    second[: SB * BS - FIRST, :] = incident[FIRST:, :].astype(jnp.float32)
    second[SB * BS - FIRST :, :] = jnp.zeros((SB * TILE, BS), jnp.float32)
    scale = keep[...] * area[...] * (1.0 / np.pi)
    rows = [pos[a : a + 1, :] - CENTRE for a in range(3)]
    rows += [component * scale for component in direction(angles[...])]
    rows += [area[...], jnp.zeros_like(scale)]
    tile = jnp.concatenate(rows, axis=0)
    slot = lax.broadcasted_iota(jnp.int32, (CAP, NYH * NZ), 0)
    for k in range(SB):
        at = SB * BS - FIRST + k * TILE
        second[at : at + 8, :] = tile[:, k * BS : (k + 1) * BS]
        for yl in range(NYL):
            slab = ((k // NC) * NYL + yl) * NC + k % NC
            live = slot < counts[slab : slab + 1, :]
            marked = jnp.where(live, lists[slab], -1).astype(jnp.float32)
            second[at + 8 + yl * CAP : at + 8 + (yl + 1) * CAP, : NYH * NZ] = marked
    rows = [recv_pos[a : a + 1, :] - CENTRE for a in range(3)]
    rows += direction(recv_angles[...])
    rows += [jnp.zeros((2, BS), jnp.float32)]
    tile = jnp.concatenate(rows, axis=0)
    for j in range(NJ):
        recv_tile[j] = tile


def prepare(me, parts, sf, ss, sd, em, lists):
    mats = selections(1)
    count = len(parts)
    for d, (first, second) in enumerate(parts):
        for k in range(SB):
            ref, start = (first, k * BS) if k * BS < FIRST else (second, k * BS - FIRST)
            em[d * SB + k] = ref[start : start + BS, :].astype(jnp.bfloat16)
        at = SB * BS - FIRST
        tiles = [second[at + k * TILE : at + k * TILE + 8, :] for k in range(SB)]
        q = split_pieces(jnp.concatenate(tiles, axis=1))
        list_at = pl.multiple_of(at + me[0] * TILE + 8, 8)
        lists[d] = second[pl.ds(list_at, 8), :].astype(jnp.int32)
        for m, out in zip(mats, (sf, ss, sd)):
            values = dot(m, q).astype(jnp.bfloat16)
            for k in range(SB):
                out[d * SB + k] = values[:, k * BS : (k + 1) * BS]
    null = count * SB
    em[null] = jnp.zeros((BS, BS), jnp.bfloat16)
    sf[null] = jnp.zeros((KF, BS), jnp.bfloat16)
    ss[null] = jnp.zeros((KS, BS), jnp.bfloat16)
    first_row = lax.broadcasted_iota(jnp.int32, (KD, BS), 0) == 0
    sd[null] = jnp.where(first_row, 1.0, 0.0).astype(jnp.bfloat16)


def src_prep_kernel(count, me, *refs):
    prepare(me, list(zip(refs[: 2 * count : 2], refs[1 : 2 * count : 2])), *refs[2 * count :])


def recv_prep_kernel(tiles, rf, rs, rd):
    mats = selections(0)
    for j in range(NJ):
        q = split_pieces(tiles[j])
        for m, ref in zip(mats, (rf, rs, rd)):
            ref[j] = lax.dot_general(
                q, m, (((0,), (1,)), ((), ())), preferred_element_type=jnp.float32
            ).astype(jnp.bfloat16)


def sweep_kernel(count, blocks, added, distance, my_y, lists, rf, rs, rd, sf, ss, sd, em, *refs):
    *before, out, ids, owner = refs
    null = sf.shape[0] - 1
    slots = count * CAP // 2

    def block_of(j):
        target = (my_y[0] + distance + (j >> 3)) & (NY - 1)
        return ((target & (NYL - 1)) * NYH + (target >> 1)) * NZ + (j & (NZ - 1))

    for j in range(blocks):
        start = jnp.zeros((BS, BS), jnp.float32)
        if added:
            start = before[0][(distance - 1) * NZ + j]
        if added == 2 and j >= HALF:
            start = start + before[1][j - HALF]
        out[j] = start

    def one_block(j, n):
        block = block_of(j)
        row = (block >> 4) * CAP
        lane = block & (NYH * NZ - 1)
        for t in range(slots):
            owner[n // 2 + t] = j
        for d in range(count):
            used = []
            for c in range(CAP):
                value = lists[d, row + c, lane]
                ids[n + c] = d * SB + value
                used.append((value >= 0).astype(jnp.int32))
            n = n + ((used[0] + used[1]) + (used[2] + used[3]))
        ids[n] = null
        return n + n % 2

    n = lax.fori_loop(0, blocks, one_block, 0)
    for t in range(2 * TAIL):
        ids[n + t] = null
    for t in range(TAIL):
        owner[n // 2 + t] = 0

    def front(u):
        a, b = ids[2 * u], ids[2 * u + 1]
        j = block_of(owner[u])

        def pair(ref):
            return jnp.concatenate([ref[a], ref[b]], axis=1)

        facing = jnp.maximum(dot(rf[j], pair(sf)), 0.0)
        seen = jnp.maximum(dot(rs[j], pair(ss)), 0.0)
        spread = dot(rd[j], pair(sd))
        return (facing * seen / (spread * spread)).astype(jnp.bfloat16)

    def back(u, values):
        a, b = ids[2 * u], ids[2 * u + 1]
        j = owner[u]
        out[j] = out[j] + dot(values, jnp.concatenate([em[a], em[b]], axis=0))

    def run(first_unit, width, steps):
        def step(i, carry):
            units = [first_unit + i * width + r for r in range(width)]
            values = [front(u) for u in units]
            for u, value in zip(units, values):
                back(u, value)
            return carry

        lax.fori_loop(0, steps, step, 0)

    units = n // 2
    long = units // UNROLL
    run(0, UNROLL, long)
    run(long * UNROLL, TAIL, pl.cdiv(units - long * UNROLL, TAIL))


VMEM_SPEC = pl.BlockSpec(memory_space=pltpu.VMEM)
SMEM_SPEC = pl.BlockSpec(memory_space=pltpu.SMEM)
BF16 = jnp.bfloat16
PARAMS = pltpu.CompilerParams(vmem_limit_bytes=VMEM_LIMIT)


def bf16_shape(*shape):
    return jax.ShapeDtypeStruct(shape, BF16)


def src_prep(me, parts):
    count = len(parts)
    rows = count * SB + 1
    return pl.pallas_call(
        functools.partial(src_prep_kernel, count),
        out_shape=[
            bf16_shape(rows, KF, BS),
            bf16_shape(rows, KS, BS),
            bf16_shape(rows, KD, BS),
            bf16_shape(rows, BS, BS),
            jax.ShapeDtypeStruct((count, 8, BS), jnp.int32),
        ],
        in_specs=[SMEM_SPEC] + [VMEM_SPEC] * (2 * count),
        out_specs=[VMEM_SPEC] * 5,
        name="src_prep",
        compiler_params=PARAMS,
        cost_estimate=pl.CostEstimate(flops=10**6, bytes_accessed=10**6, transcendentals=0),
    )(me, *[part for pair in parts for part in pair])


def recv_prep(tiles):
    return pl.pallas_call(
        recv_prep_kernel,
        out_shape=[bf16_shape(NJ, BS, KF), bf16_shape(NJ, BS, KS), bf16_shape(NJ, BS, KD)],
        in_specs=[VMEM_SPEC],
        out_specs=[VMEM_SPEC] * 3,
        name="recv_prep",
        compiler_params=PARAMS,
        cost_estimate=pl.CostEstimate(flops=10**6, bytes_accessed=10**6, transcendentals=0),
    )(tiles)


def sweep(my_y, distance, recv, src, count, blocks, *before):
    *src, lists = src
    return pl.pallas_call(
        functools.partial(sweep_kernel, count, blocks, len(before), distance),
        out_shape=jax.ShapeDtypeStruct((blocks, BS, BS), jnp.float32),
        in_specs=[SMEM_SPEC] * 2 + [VMEM_SPEC] * (7 + len(before)),
        out_specs=VMEM_SPEC,
        scratch_shapes=[
            pltpu.SMEM((blocks * count * CAP + 4 * UNROLL,), jnp.int32),
            pltpu.SMEM((blocks * count * CAP // 2 + count * CAP + 2 * UNROLL,), jnp.int32),
        ],
        name="sweep",
        compiler_params=PARAMS,
        cost_estimate=pl.CostEstimate(flops=10**6, bytes_accessed=10**6, transcendentals=0),
    )(my_y, lists, *recv, *src, *before)


def pack(*operands):
    return pl.pallas_call(
        pack_kernel,
        out_shape=[
            jax.ShapeDtypeStruct((FIRST, BS), jnp.float32),
            jax.ShapeDtypeStruct((SB * (BS + TILE) - FIRST, BS), jnp.float32),
            jax.ShapeDtypeStruct((NJ, 8, BS), jnp.float32),
        ],
        in_specs=[VMEM_SPEC] * 9,
        out_specs=[VMEM_SPEC] * 3,
        name="pack",
        compiler_params=pltpu.CompilerParams(vmem_limit_bytes=60 << 20),
        cost_estimate=pl.CostEstimate(flops=10**6, bytes_accessed=10**6, transcendentals=0),
    )(*operands)


def y_route(distance):
    def linear(y):
        return (y % NYL) * NYH + y // NYL

    return [(linear(y), linear((y + distance) % NY)) for y in range(NY)]


def shards(
    recv_pos,
    recv_angles,
    src_pos,
    src_angles,
    src_area,
    reemission,
    incident,
    direct,
    visible_lists,
    visible_counts,
):
    *mine, recv_tile = pack(
        incident,
        src_pos,
        src_angles,
        src_area.reshape(1, SB * BS),
        reemission.reshape(1, SB * BS),
        visible_lists[0, 0].transpose(0, 2, 1),
        visible_counts[0, 0],
        recv_pos,
        recv_angles,
    )

    def along_x(block, distance):
        return lax.ppermute(block, "x", [(i, (i + distance) % NX) for i in range(NX)])

    def other_core(block):
        return lax.ppermute(block, "c", [(0, 1), (1, 0)])

    me = (lax.axis_index("x") * NC + lax.axis_index("c")).astype(jnp.int32).reshape(1)
    my_y = (lax.axis_index("yh") * NYL + lax.axis_index("yl")).astype(jnp.int32).reshape(1)
    left = [along_x(mine[0], 1), None]
    right = [None, along_x(mine[1], 3)]
    left[1], right[0] = along_x(mine[1], 1), along_x(mine[0], 3)
    own = [other_core(part) for part in mine]

    tiles = lax.all_to_all(recv_tile, ("yl", "yh", "z"), 0, 0, tiled=True)

    *left, right[0], right[1], own[0], own[1], tiles = lax.optimization_barrier(
        (*left, *right, *own, tiles)
    )
    far = [along_x(left[0], 1), along_x(right[1], 3)]
    sides = [left, right] + [[other_core(part) for part in pair] for pair in (left, right)]

    recv = recv_prep(tiles)
    begun = sweep(my_y, 1, recv, src_prep(me, [mine, own]), 2, 3 * NZ)
    *far, begun = lax.optimization_barrier((*far, begun))
    src = src_prep(me, sides + [far, [other_core(part) for part in far]] + [mine, own])

    def along_y(block, distance):
        return lax.ppermute(block, ("yl", "yh"), y_route(distance))

    def part(distance, *passing):
        return sweep(my_y, distance, recv, src, GROUP - 2, NZ, begun, *passing)

    across = part(2)
    by_left, by_right = along_y(across[:HALF], 1), along_y(across[HALF:], 3)
    ahead = part(1)
    ahead = along_y(jnp.concatenate([ahead[:HALF] + by_left, ahead[HALF:]], axis=0), 1)
    behind = along_y(part(3, by_right), 3)
    total = sweep(my_y, 0, recv, src, GROUP, NZ) + ahead + behind
    pieces = lax.all_to_all(total, "z", 0, 0, tiled=True)
    return direct + jnp.sum(pieces, axis=0)


def solution(mesh):
    fine = Mesh(mesh.devices.reshape(NX, NYL, NC, NYH, NZ), ("x", "yl", "c", "yh", "z"))
    blk, lane = ("x", "yl", "c"), ("yh", "z")
    both = blk + lane
    return jax.shard_map(
        shards,
        mesh=fine,
        in_specs=(
            P(None, both),
            P(None, both),
            P(None, both),
            P(None, both),
            P(both),
            P(both),
            P(both, None),
            P(both, None),
            P(blk, lane, None, None, None),
            P(blk, lane, None, None),
        ),
        out_specs=P(both, None),
        check_vma=False,
    )
```

```python
import functools

import jax
import jax.numpy as jnp
import numpy as np
from jax import lax
from jax.experimental import pallas as pl
from jax.experimental.pallas import tpu as pltpu
from jax.sharding import Mesh
from jax.sharding import PartitionSpec as P

NX, NYL, NC, NYH, NZ = 4, 2, 2, 2, 8
NY = NYL * NYH
BS = 128
SB = 8
CAP = 4
GROUP = NX * NC
NJ = NY * NZ
CENTRE = 3.0
TILE = 16
POS, NRM, AREA = 0, 3, 6
ROWS, DOT, SQA, SQB, ONE = 16, 8, 9, 10, 11
KF, KS, KD = 32, 32, 48
VMEM_LIMIT = 16 << 20
UNROLL, TAIL = 16, 8
FLUX = SB * BS


def contraction_terms():
    pieces = [(i, j) for i in range(3) for j in range(3) if i + j < 4]

    def product(scale, rrow, srow):
        return [
            (scale, i * ROWS + rrow + a, j * ROWS + srow + a) for i, j in pieces for a in range(3)
        ]

    def from_recv(row, count):
        return [(1.0, i * ROWS + row, ONE) for i in range(count)]

    def from_src(row, count):
        return [(1.0, ONE, i * ROWS + row) for i in range(count)]

    facing = product(1.0, NRM, POS) + from_recv(DOT, 3)
    seen = product(1.0, POS, NRM) + from_src(DOT, 3)
    cross = product(-2.0, POS, POS)
    spread = (
        from_src(SQA, 2) + from_recv(SQA, 2) + cross + from_recv(SQB, 3) + from_src(SQB, 3)
    )
    return (KF, facing), (KS, seen), (KD, spread)


def selections(side):
    made = []
    for depth, terms in contraction_terms():
        groups = []
        for start in range(0, depth, 8):
            row = lax.broadcasted_iota(jnp.int32, (8, 3 * ROWS), 0)
            column = lax.broadcasted_iota(jnp.int32, (8, 3 * ROWS), 1)
            group = jnp.zeros((8, 3 * ROWS), jnp.float32)
            for at, term in enumerate(terms[start : start + 8]):
                value = term[0] if side == 0 else 1.0
                here = (row == at) & (column == term[1 + side])
                group = jnp.where(here, value, group)
            groups.append(group)
        made.append(jnp.concatenate(groups, axis=0).astype(jnp.bfloat16))
    return made


def split_pieces(tile):
    row = lax.broadcasted_iota(jnp.int32, tile.shape, 0)
    fixed = row < NRM
    coarse = jnp.where(fixed, jnp.round(tile * 32.0) * (1.0 / 32.0), tile)
    along = -(
        tile[NRM : NRM + 1] * tile[POS : POS + 1]
        + tile[NRM + 1 : NRM + 2] * tile[POS + 1 : POS + 2]
        + tile[NRM + 2 : NRM + 3] * tile[POS + 2 : POS + 3]
    )
    grid = [coarse[a : a + 1] for a in range(3)]
    fine = [tile[a : a + 1] - grid[a] for a in range(3)]
    square_a = grid[0] * grid[0] + grid[1] * grid[1] + grid[2] * grid[2]
    square_b = (
        fine[0] * (2.0 * grid[0] + fine[0])
        + fine[1] * (2.0 * grid[1] + fine[1])
        + fine[2] * (2.0 * grid[2] + fine[2])
    ) + tile[AREA : AREA + 1]
    derived = jnp.where(
        row == 0,
        along,
        jnp.where(
            row == 1, square_a, jnp.where(row == 2, square_b, jnp.where(row == 3, 1.0, 0.0))
        ),
    )
    values = jnp.concatenate([tile, derived], axis=0)
    high = jnp.concatenate([coarse, derived], axis=0).astype(jnp.bfloat16)
    rest = values - high.astype(jnp.float32)
    cut = lax.broadcasted_iota(jnp.int32, values.shape, 0) < NRM
    mid = jnp.where(cut, jnp.round(rest * 8192.0) * (1.0 / 8192.0), rest).astype(jnp.bfloat16)
    low = (rest - mid.astype(jnp.float32)).astype(jnp.bfloat16)
    return jnp.concatenate([high, mid, low], axis=0)


def dot(a, b):
    return jnp.dot(a, b, preferred_element_type=jnp.float32)


def direction(angles):
    polar, azimuth = angles[0:1], angles[1:2]
    across = jnp.sin(polar)
    return [across * jnp.cos(azimuth), across * jnp.sin(azimuth), jnp.cos(polar)]


def pack_kernel(
    incident, pos, angles, area, keep, lists, counts, recv_pos, recv_angles, packed, recv_tile
):
    packed[:FLUX, :] = incident[...].astype(jnp.float32)
    packed[FLUX:, :] = jnp.zeros((SB * TILE, BS), jnp.float32)
    scale = keep[...] * area[...] * (1.0 / np.pi)
    rows = [pos[a : a + 1, :] - CENTRE for a in range(3)]
    rows += [component * scale for component in direction(angles[...])]
    rows += [area[...], jnp.zeros_like(scale)]
    tile = jnp.concatenate(rows, axis=0)
    slot = lax.broadcasted_iota(jnp.int32, (CAP, NYH * NZ), 0)
    for k in range(SB):
        at = FLUX + k * TILE
        packed[at : at + 8, :] = tile[:, k * BS : (k + 1) * BS]
        for yl in range(NYL):
            slab = ((k // NC) * NYL + yl) * NC + k % NC
            live = slot < counts[slab : slab + 1, :]
            marked = jnp.where(live, lists[slab], -1).astype(jnp.float32)
            packed[at + 8 + yl * CAP : at + 8 + (yl + 1) * CAP, : NYH * NZ] = marked
    rows = [recv_pos[a : a + 1, :] - CENTRE for a in range(3)]
    rows += direction(recv_angles[...])
    rows += [jnp.zeros((2, BS), jnp.float32)]
    tile = jnp.concatenate(rows, axis=0)
    for j in range(NJ):
        recv_tile[j] = tile


def src_prep_kernel(count, me, *refs):
    packed = refs[:count]
    sf, ss, sd, em, lists = refs[count:]
    mats = selections(1)
    for d, ref in enumerate(packed):
        for k in range(SB):
            em[d * SB + k] = ref[k * BS : (k + 1) * BS, :].astype(jnp.bfloat16)
        tiles = [ref[FLUX + k * TILE : FLUX + k * TILE + 8, :] for k in range(SB)]
        q = split_pieces(jnp.concatenate(tiles, axis=1))
        list_at = pl.multiple_of(FLUX + me[0] * TILE + 8, 8)
        lists[d] = ref[pl.ds(list_at, 8), :].astype(jnp.int32)
        for m, out in zip(mats, (sf, ss, sd)):
            values = dot(m, q).astype(jnp.bfloat16)
            for k in range(SB):
                out[d * SB + k] = values[:, k * BS : (k + 1) * BS]
    null = count * SB
    em[null] = jnp.zeros((BS, BS), jnp.bfloat16)
    sf[null] = jnp.zeros((KF, BS), jnp.bfloat16)
    ss[null] = jnp.zeros((KS, BS), jnp.bfloat16)
    first_row = lax.broadcasted_iota(jnp.int32, (KD, BS), 0) == 0
    sd[null] = jnp.where(first_row, 1.0, 0.0).astype(jnp.bfloat16)


def recv_prep_kernel(tiles, rf, rs, rd):
    mats = selections(0)
    for j in range(NJ):
        q = split_pieces(tiles[j])
        for m, ref in zip(mats, (rf, rs, rd)):
            ref[j] = lax.dot_general(
                q, m, (((0,), (1,)), ((), ())), preferred_element_type=jnp.float32
            ).astype(jnp.bfloat16)


def sweep_kernel(count, distances, added, sizes, my_y, lists, rf, rs, rd, sf, ss, sd, em, *refs):
    before, outs = refs[:added], refs[added:-3]
    out, ids, owner = refs[-3:]
    blocks = len(distances) * NZ
    null = sf.shape[0] - 1
    slots = count * CAP // 2

    def block_of(j):
        ahead = distances[0]
        for at in range(1, len(distances)):
            ahead = jnp.where(j >= at * NZ, distances[at], ahead)
        target = (my_y[0] + ahead) & (NY - 1)
        return ((target & (NYL - 1)) * NYH + (target >> 1)) * NZ + (j & (NZ - 1))

    for j in range(blocks):
        start = jnp.zeros((BS, BS), jnp.float32)
        if added:
            start = before[0][(distances[j // NZ] - 1) * NZ + j % NZ]
        out[j] = start

    def one_block(j, n):
        block = block_of(j)
        row = (block >> 4) * CAP
        lane = block & (NYH * NZ - 1)
        for t in range(slots):
            owner[n // 2 + t] = j
        for d in range(count):
            used = []
            for c in range(CAP):
                value = lists[d, row + c, lane]
                ids[n + c] = d * SB + value
                used.append((value >= 0).astype(jnp.int32))
            n = n + ((used[0] + used[1]) + (used[2] + used[3]))
        ids[n] = null
        return n + n % 2

    n = lax.fori_loop(0, blocks, one_block, 0)
    for t in range(2 * TAIL):
        ids[n + t] = null
    for t in range(TAIL):
        owner[n // 2 + t] = 0

    def front(u):
        a, b = ids[2 * u], ids[2 * u + 1]
        j = block_of(owner[u])

        def pair(ref):
            return jnp.concatenate([ref[a], ref[b]], axis=1)

        facing = jnp.maximum(dot(rf[j], pair(sf)), 0.0)
        seen = jnp.maximum(dot(rs[j], pair(ss)), 0.0)
        spread = dot(rd[j], pair(sd))
        return (facing * seen / (spread * spread)).astype(jnp.bfloat16)

    def back(u, values):
        a, b = ids[2 * u], ids[2 * u + 1]
        j = owner[u]
        out[j] = out[j] + dot(values, jnp.concatenate([em[a], em[b]], axis=0))

    def run(first_unit, width, steps):
        def step(i, carry):
            units = [first_unit + i * width + r for r in range(width)]
            values = [front(u) for u in units]
            for u, value in zip(units, values):
                back(u, value)
            return carry

        lax.fori_loop(0, steps, step, 0)

    units = n // 2
    long = units // UNROLL
    run(0, UNROLL, long)
    run(long * UNROLL, TAIL, pl.cdiv(units - long * UNROLL, TAIL))
    at = 0
    for ref, size in zip(outs, sizes):
        ref[...] = out[at : at + size]
        at += size


VMEM_SPEC = pl.BlockSpec(memory_space=pltpu.VMEM)
SMEM_SPEC = pl.BlockSpec(memory_space=pltpu.SMEM)
BF16 = jnp.bfloat16
PARAMS = pltpu.CompilerParams(vmem_limit_bytes=VMEM_LIMIT)


def bf16_shape(*shape):
    return jax.ShapeDtypeStruct(shape, BF16)


def src_prep(me, packed):
    count = len(packed)
    rows = count * SB + 1
    return pl.pallas_call(
        functools.partial(src_prep_kernel, count),
        out_shape=[
            bf16_shape(rows, KF, BS),
            bf16_shape(rows, KS, BS),
            bf16_shape(rows, KD, BS),
            bf16_shape(rows, BS, BS),
            jax.ShapeDtypeStruct((count, 8, BS), jnp.int32),
        ],
        in_specs=[SMEM_SPEC] + [VMEM_SPEC] * count,
        out_specs=[VMEM_SPEC] * 5,
        name="src_prep",
        compiler_params=PARAMS,
        cost_estimate=pl.CostEstimate(flops=10**6, bytes_accessed=10**6, transcendentals=0),
    )(me, *packed)


def recv_prep(tiles):
    return pl.pallas_call(
        recv_prep_kernel,
        out_shape=[bf16_shape(NJ, BS, KF), bf16_shape(NJ, BS, KS), bf16_shape(NJ, BS, KD)],
        in_specs=[VMEM_SPEC],
        out_specs=[VMEM_SPEC] * 3,
        name="recv_prep",
        compiler_params=PARAMS,
        cost_estimate=pl.CostEstimate(flops=10**6, bytes_accessed=10**6, transcendentals=0),
    )(tiles)


def sweep(my_y, distances, recv, src, count, *before, sizes=None):
    *src, lists = src
    blocks = len(distances) * NZ
    sizes = sizes or (blocks,)
    return pl.pallas_call(
        functools.partial(sweep_kernel, count, distances, len(before), sizes),
        out_shape=[jax.ShapeDtypeStruct((size, BS, BS), jnp.float32) for size in sizes],
        in_specs=[SMEM_SPEC] * 2 + [VMEM_SPEC] * (7 + len(before)),
        out_specs=[VMEM_SPEC] * len(sizes),
        scratch_shapes=[
            pltpu.VMEM((blocks, BS, BS), jnp.float32),
            pltpu.SMEM((blocks * count * CAP + 4 * UNROLL,), jnp.int32),
            pltpu.SMEM((blocks * count * CAP // 2 + count * CAP + 2 * UNROLL,), jnp.int32),
        ],
        name="sweep",
        compiler_params=PARAMS,
        cost_estimate=pl.CostEstimate(flops=10**6, bytes_accessed=10**6, transcendentals=0),
    )(my_y, lists, *recv, *src, *before)


def pack(*operands):
    return pl.pallas_call(
        pack_kernel,
        out_shape=[
            jax.ShapeDtypeStruct((FLUX + SB * TILE, BS), jnp.float32),
            jax.ShapeDtypeStruct((NJ, 8, BS), jnp.float32),
        ],
        in_specs=[VMEM_SPEC] * 9,
        out_specs=[VMEM_SPEC] * 2,
        name="pack",
        compiler_params=pltpu.CompilerParams(vmem_limit_bytes=60 << 20),
        cost_estimate=pl.CostEstimate(flops=10**6, bytes_accessed=10**6, transcendentals=0),
    )(*operands)


def y_route(distance):
    def linear(y):
        return (y % NYL) * NYH + y // NYL

    return [(linear(y), linear((y + distance) % NY)) for y in range(NY)]


def shards(
    recv_pos,
    recv_angles,
    src_pos,
    src_angles,
    src_area,
    reemission,
    incident,
    direct,
    visible_lists,
    visible_counts,
):
    mine, recv_tile = pack(
        incident,
        src_pos,
        src_angles,
        src_area.reshape(1, SB * BS),
        reemission.reshape(1, SB * BS),
        visible_lists[0, 0].transpose(0, 2, 1),
        visible_counts[0, 0],
        recv_pos,
        recv_angles,
    )

    def along_x(block, distance):
        return lax.ppermute(block, "x", [(i, (i + distance) % NX) for i in range(NX)])

    def other_core(block):
        return lax.ppermute(block, "c", [(0, 1), (1, 0)])

    me = (lax.axis_index("x") * NC + lax.axis_index("c")).astype(jnp.int32).reshape(1)
    my_y = (lax.axis_index("yh") * NYL + lax.axis_index("yl")).astype(jnp.int32).reshape(1)
    far = [along_x(mine, distance) for distance in (1, 3, 2)]
    own = other_core(mine)

    tiles = lax.all_to_all(recv_tile, ("yl", "yh", "z"), 0, 0, tiled=True)

    own, tiles = lax.optimization_barrier((own, tiles))
    recv = recv_prep(tiles)
    (begun,) = sweep(my_y, (1, 2, 3), recv, src_prep(me, [mine, own]), 2)
    *far, begun = lax.optimization_barrier((*far, begun))
    src = src_prep(me, far + [other_core(block) for block in far] + [mine, own])

    def along_y(block, distance):
        return lax.ppermute(block, ("yl", "yh"), y_route(distance))

    half = NZ // 2
    parts = sweep(my_y, (2,), recv, src, GROUP - 2, begun, sizes=(half, half))
    by_left, by_right = along_y(parts[0], 1), along_y(parts[1], 3)
    ahead, behind = sweep(my_y, (1, 3), recv, src, GROUP - 2, begun, sizes=(NZ, NZ))
    ahead = along_y(ahead.at[:half].add(by_left), 1)
    behind = along_y(behind.at[half:].add(by_right), 3)
    (total,) = sweep(my_y, (0,), recv, src, GROUP)
    total = total + ahead + behind
    pieces = lax.all_to_all(total, "z", 0, 0, tiled=True)
    return direct + jnp.sum(pieces, axis=0)


def solution(mesh):
    fine = Mesh(mesh.devices.reshape(NX, NYL, NC, NYH, NZ), ("x", "yl", "c", "yh", "z"))
    blk, lane = ("x", "yl", "c"), ("yh", "z")
    both = blk + lane
    return jax.shard_map(
        shards,
        mesh=fine,
        in_specs=(
            P(None, both),
            P(None, both),
            P(None, both),
            P(None, both),
            P(both),
            P(both),
            P(both, None),
            P(both, None),
            P(blk, lane, None, None, None),
            P(blk, lane, None, None),
        ),
        out_specs=P(both, None),
        check_vma=False,
    )
```

```python
import functools

import jax
import jax.numpy as jnp
import numpy as np
from jax import lax
from jax.experimental import pallas as pl
from jax.experimental.pallas import tpu as pltpu
from jax.sharding import Mesh
from jax.sharding import PartitionSpec as P

NX, NYL, NC, NYH, NZ = 4, 2, 2, 2, 8
NY = NYL * NYH
BS = 128
SB = 8
CAP = 4
GROUP = NX * NC
NJ = NY * NZ
CENTRE = 3.0
TILE = 8
POS, NRM, AREA = 0, 3, 6
ROWS, DOT, SQA, SQB, ONE = 16, 8, 9, 10, 11
KF, KS, KD = 32, 32, 48
VMEM_LIMIT = 16 << 20
UNROLL, TAIL = 16, 8
FLUX = SB * BS
LISTS = FLUX + SB * TILE
LANES = NYH * NZ
TABLE = 40
COUNT = GROUP * CAP


def contraction_terms():
    pieces = [(i, j) for i in range(3) for j in range(3) if i + j < 4]

    def product(scale, rrow, srow):
        return [
            (scale, i * ROWS + rrow + a, j * ROWS + srow + a) for i, j in pieces for a in range(3)
        ]

    def from_recv(row, count):
        return [(1.0, i * ROWS + row, ONE) for i in range(count)]

    def from_src(row, count):
        return [(1.0, ONE, i * ROWS + row) for i in range(count)]

    facing = product(1.0, NRM, POS) + from_recv(DOT, 3)
    seen = product(1.0, POS, NRM) + from_src(DOT, 3)
    cross = product(-2.0, POS, POS)
    spread = (
        from_src(SQA, 2) + from_recv(SQA, 2) + cross + from_recv(SQB, 3) + from_src(SQB, 3)
    )
    return (KF, facing), (KS, seen), (KD, spread)


def selections(side):
    made = []
    for depth, terms in contraction_terms():
        groups = []
        for start in range(0, depth, 8):
            row = lax.broadcasted_iota(jnp.int32, (8, 3 * ROWS), 0)
            column = lax.broadcasted_iota(jnp.int32, (8, 3 * ROWS), 1)
            group = jnp.zeros((8, 3 * ROWS), jnp.float32)
            for at, term in enumerate(terms[start : start + 8]):
                value = term[0] if side == 0 else 1.0
                here = (row == at) & (column == term[1 + side])
                group = jnp.where(here, value, group)
            groups.append(group)
        made.append(jnp.concatenate(groups, axis=0).astype(jnp.bfloat16))
    return made


def split_pieces(tile):
    row = lax.broadcasted_iota(jnp.int32, tile.shape, 0)
    fixed = row < NRM
    coarse = jnp.where(fixed, jnp.round(tile * 32.0) * (1.0 / 32.0), tile)
    along = -(
        tile[NRM : NRM + 1] * tile[POS : POS + 1]
        + tile[NRM + 1 : NRM + 2] * tile[POS + 1 : POS + 2]
        + tile[NRM + 2 : NRM + 3] * tile[POS + 2 : POS + 3]
    )
    grid = [coarse[a : a + 1] for a in range(3)]
    fine = [tile[a : a + 1] - grid[a] for a in range(3)]
    square_a = grid[0] * grid[0] + grid[1] * grid[1] + grid[2] * grid[2]
    square_b = (
        fine[0] * (2.0 * grid[0] + fine[0])
        + fine[1] * (2.0 * grid[1] + fine[1])
        + fine[2] * (2.0 * grid[2] + fine[2])
    ) + tile[AREA : AREA + 1]
    derived = jnp.where(
        row == 0,
        along,
        jnp.where(
            row == 1, square_a, jnp.where(row == 2, square_b, jnp.where(row == 3, 1.0, 0.0))
        ),
    )
    values = jnp.concatenate([tile, derived], axis=0)
    high = jnp.concatenate([coarse, derived], axis=0).astype(jnp.bfloat16)
    rest = values - high.astype(jnp.float32)
    cut = lax.broadcasted_iota(jnp.int32, values.shape, 0) < NRM
    mid = jnp.where(cut, jnp.round(rest * 8192.0) * (1.0 / 8192.0), rest).astype(jnp.bfloat16)
    low = (rest - mid.astype(jnp.float32)).astype(jnp.bfloat16)
    return jnp.concatenate([high, mid, low], axis=0)


def dot(a, b):
    return jnp.dot(a, b, preferred_element_type=jnp.float32)


def direction(angles):
    polar, azimuth = angles[0:1], angles[1:2]
    across = jnp.sin(polar)
    return [across * jnp.cos(azimuth), across * jnp.sin(azimuth), jnp.cos(polar)]


def pack_kernel(
    incident, pos, angles, area, keep, lists, counts, recv_pos, recv_angles, packed, recv_tile
):
    packed[:FLUX, :] = incident[...].astype(jnp.float32)
    scale = keep[...] * area[...] * (1.0 / np.pi)
    rows = [pos[a : a + 1, :] - CENTRE for a in range(3)]
    rows += [component * scale for component in direction(angles[...])]
    rows += [area[...], jnp.zeros_like(scale)]
    tile = jnp.concatenate(rows, axis=0)
    slot = lax.broadcasted_iota(jnp.int32, (CAP, LANES), 0)
    for k in range(SB):
        packed[FLUX + k * TILE : FLUX + (k + 1) * TILE, :] = tile[:, k * BS : (k + 1) * BS]
    for k in range(GROUP):
        for yl in range(NYL):
            slab = ((k // NC) * NYL + yl) * NC + k % NC
            live = slot < counts[slab : slab + 1, :]
            marked = jnp.where(live, lists[slab], -1).astype(jnp.float32)
            rows = slice(LISTS + yl * CAP, LISTS + (yl + 1) * CAP)
            packed[rows, k * LANES : (k + 1) * LANES] = marked
    rows = [recv_pos[a : a + 1, :] - CENTRE for a in range(3)]
    rows += direction(recv_angles[...])
    rows += [jnp.zeros((2, BS), jnp.float32)]
    tile = jnp.concatenate(rows, axis=0)
    for j in range(NJ):
        recv_tile[j] = tile


def compact(count, first, packed, table):
    place = lax.broadcasted_iota(jnp.int32, (COUNT, BS), 0)
    for yl in range(NYL):
        entries = jnp.full((COUNT, BS), count * SB, jnp.int32)
        filled = jnp.zeros((1, BS), jnp.int32)
        for d in range(count):
            if d == first:
                table[yl * TABLE + COUNT : yl * TABLE + COUNT + 1, :] = filled
            for c in range(CAP):
                at = LISTS + yl * CAP + c
                value = packed[d][at : at + 1, :].astype(jnp.int32)
                live = value >= 0
                entries = jnp.where(place == jnp.where(live, filled, -1), value + d * SB, entries)
                filled = filled + live.astype(jnp.int32)
        table[yl * TABLE : yl * TABLE + COUNT, :] = entries
        table[yl * TABLE + COUNT + 1 : yl * TABLE + COUNT + 2, :] = filled


def src_prep_kernel(count, first, *refs):
    packed = refs[:count]
    sf, ss, sd, em, table = refs[count:]
    mats = selections(1)
    table[...] = jnp.zeros(table.shape, jnp.int32)
    compact(count, first, packed, table)
    for d, ref in enumerate(packed):
        for k in range(SB):
            em[d * SB + k] = ref[k * BS : (k + 1) * BS, :].astype(jnp.bfloat16)
        tiles = [ref[FLUX + k * TILE : FLUX + (k + 1) * TILE, :] for k in range(SB)]
        q = split_pieces(jnp.concatenate(tiles, axis=1))
        for m, out in zip(mats, (sf, ss, sd)):
            values = dot(m, q).astype(jnp.bfloat16)
            for k in range(SB):
                out[d * SB + k] = values[:, k * BS : (k + 1) * BS]
    null = count * SB
    em[null] = jnp.zeros((BS, BS), jnp.bfloat16)
    sf[null] = jnp.zeros((KF, BS), jnp.bfloat16)
    ss[null] = jnp.zeros((KS, BS), jnp.bfloat16)
    first_row = lax.broadcasted_iota(jnp.int32, (KD, BS), 0) == 0
    sd[null] = jnp.where(first_row, 1.0, 0.0).astype(jnp.bfloat16)


def recv_prep_kernel(tiles, rf, rs, rd):
    mats = selections(0)
    for j in range(NJ):
        q = split_pieces(tiles[j])
        for m, ref in zip(mats, (rf, rs, rd)):
            ref[j] = lax.dot_general(
                q, m, (((0,), (1,)), ((), ())), preferred_element_type=jnp.float32
            ).astype(jnp.bfloat16)


def sweep_kernel(most, whole, distances, added, sizes, place, table, rf, rs, rd, sf, ss, sd, em, *refs):
    before, outs = refs[:added], refs[added:-2]
    out, codes = refs[-2:]
    null = sf.shape[0] - 1
    my_y, lane = place[0], place[1] * LANES

    for j in range(len(distances) * NZ):
        start = jnp.zeros((BS, BS), jnp.float32)
        if added:
            start = before[0][(distances[j // NZ] - 1) * NZ + j % NZ]
        out[j] = start

    n = jnp.int32(0)
    for at, distance in enumerate(distances):
        target = (my_y + distance) & (NY - 1)
        base = ((target & (NYL - 1)) * NYH + (target >> 1)) * NZ

        def one_block(z, n, at=at, base=base):
            block = base + z
            used = table[(block >> 4) * TABLE + COUNT + int(whole), lane + (block & (LANES - 1))]
            code = (block << 8) | ((z + at * NZ) << 16)
            for t in range(most * CAP // 2):
                codes[n + t] = code + t
            units = (used + 1) >> 1
            last = jnp.maximum(units - 1, 0)
            codes[n + last] = (code + last) | ((used & 1) << 24)
            return n + units

        n = lax.fori_loop(0, NZ, one_block, n)
    for t in range(TAIL):
        codes[n + t] = 3 << 24

    def decode(u):
        code = codes[u]
        block = (code >> 8) & 255
        row = (block >> 4) * TABLE + 2 * (code & 255)
        column = lane + (block & (LANES - 1))
        a = jnp.where(code >= 2 << 24, null, table[row, column])
        b = jnp.where(code >= 1 << 24, null, table[row + 1, column])
        return a, b, block, (code >> 16) & 255

    def front(a, b, block, j):
        def pair(ref):
            return jnp.concatenate([ref[a], ref[b]], axis=1)

        facing = jnp.maximum(dot(rf[block], pair(sf)), 0.0)
        seen = jnp.maximum(dot(rs[block], pair(ss)), 0.0)
        spread = dot(rd[block], pair(sd))
        return (facing * seen / (spread * spread)).astype(jnp.bfloat16)

    def run(first_unit, width, steps):
        def step(i, carry):
            units = [decode(first_unit + i * width + r) for r in range(width)]
            values = [front(*unit) for unit in units]
            for (a, b, block, j), value in zip(units, values):
                out[j] = out[j] + dot(value, jnp.concatenate([em[a], em[b]], axis=0))
            return carry

        lax.fori_loop(0, steps, step, 0)

    long = n // UNROLL
    run(0, UNROLL, long)
    run(long * UNROLL, TAIL, pl.cdiv(n - long * UNROLL, TAIL))
    at = 0
    for ref, size in zip(outs, sizes):
        ref[...] = out[at : at + size]
        at += size


VMEM_SPEC = pl.BlockSpec(memory_space=pltpu.VMEM)
SMEM_SPEC = pl.BlockSpec(memory_space=pltpu.SMEM)
BF16 = jnp.bfloat16
PARAMS = pltpu.CompilerParams(vmem_limit_bytes=VMEM_LIMIT)


def bf16_shape(*shape):
    return jax.ShapeDtypeStruct(shape, BF16)


def src_prep(packed, first):
    count = len(packed)
    rows = count * SB + 1
    return pl.pallas_call(
        functools.partial(src_prep_kernel, count, first),
        out_shape=[
            bf16_shape(rows, KF, BS),
            bf16_shape(rows, KS, BS),
            bf16_shape(rows, KD, BS),
            bf16_shape(rows, BS, BS),
            jax.ShapeDtypeStruct((NYL * TABLE, BS), jnp.int32),
        ],
        in_specs=[VMEM_SPEC] * count,
        out_specs=[VMEM_SPEC] * 5,
        name="src_prep",
        compiler_params=PARAMS,
        cost_estimate=pl.CostEstimate(flops=10**6, bytes_accessed=10**6, transcendentals=0),
    )(*packed)


def recv_prep(tiles):
    return pl.pallas_call(
        recv_prep_kernel,
        out_shape=[bf16_shape(NJ, BS, KF), bf16_shape(NJ, BS, KS), bf16_shape(NJ, BS, KD)],
        in_specs=[VMEM_SPEC],
        out_specs=[VMEM_SPEC] * 3,
        name="recv_prep",
        compiler_params=PARAMS,
        cost_estimate=pl.CostEstimate(flops=10**6, bytes_accessed=10**6, transcendentals=0),
    )(tiles)


def sweep(place, distances, recv, src, count, whole, *before, sizes=None):
    *src, table = src
    blocks = len(distances) * NZ
    sizes = sizes or (blocks,)
    return pl.pallas_call(
        functools.partial(sweep_kernel, count, whole, distances, len(before), sizes),
        out_shape=[jax.ShapeDtypeStruct((size, BS, BS), jnp.float32) for size in sizes],
        in_specs=[SMEM_SPEC] * 2 + [VMEM_SPEC] * (7 + len(before)),
        out_specs=[VMEM_SPEC] * len(sizes),
        scratch_shapes=[
            pltpu.VMEM((blocks, BS, BS), jnp.float32),
            pltpu.SMEM((blocks * count * CAP // 2 + count * CAP + UNROLL,), jnp.int32),
        ],
        name="sweep",
        compiler_params=PARAMS,
        cost_estimate=pl.CostEstimate(flops=10**6, bytes_accessed=10**6, transcendentals=0),
    )(place, table, *recv, *src, *before)


def pack(*operands):
    return pl.pallas_call(
        pack_kernel,
        out_shape=[
            jax.ShapeDtypeStruct((LISTS + TILE, BS), jnp.float32),
            jax.ShapeDtypeStruct((NJ, 8, BS), jnp.float32),
        ],
        in_specs=[VMEM_SPEC] * 9,
        out_specs=[VMEM_SPEC] * 2,
        name="pack",
        compiler_params=pltpu.CompilerParams(vmem_limit_bytes=60 << 20),
        cost_estimate=pl.CostEstimate(flops=10**6, bytes_accessed=10**6, transcendentals=0),
    )(*operands)


def y_route(distance):
    def linear(y):
        return (y % NYL) * NYH + y // NYL

    return [(linear(y), linear((y + distance) % NY)) for y in range(NY)]


def shards(
    recv_pos,
    recv_angles,
    src_pos,
    src_angles,
    src_area,
    reemission,
    incident,
    direct,
    visible_lists,
    visible_counts,
):
    mine, recv_tile = pack(
        incident,
        src_pos,
        src_angles,
        src_area.reshape(1, SB * BS),
        reemission.reshape(1, SB * BS),
        visible_lists[0, 0].transpose(0, 2, 1),
        visible_counts[0, 0],
        recv_pos,
        recv_angles,
    )

    def along_x(block, distance):
        return lax.ppermute(block, "x", [(i, (i + distance) % NX) for i in range(NX)])

    def other_core(block):
        return lax.ppermute(block, "c", [(0, 1), (1, 0)])

    my_y = lax.axis_index("yh") * NYL + lax.axis_index("yl")
    place = jnp.stack([my_y, lax.axis_index("x") * NC + lax.axis_index("c")]).astype(jnp.int32)
    far = [along_x(mine, distance) for distance in (1, 3, 2)]
    own = other_core(mine)

    tiles = lax.all_to_all(recv_tile, ("yl", "yh", "z"), 0, 0, tiled=True)

    own, tiles = lax.optimization_barrier((own, tiles))
    recv = list(recv_prep(tiles))
    left, right, recv[0] = lax.optimization_barrier((far[0], far[1], recv[0]))
    sides = [left, right, other_core(left), other_core(right)]
    near = list(src_prep([mine, own], 0))
    sides[2], sides[3], near[0] = lax.optimization_barrier((sides[2], sides[3], near[0]))
    (begun,) = sweep(place, (1, 2, 3), recv, near, 2, True)
    opposite, begun = lax.optimization_barrier((far[2], begun))
    src = src_prep(sides + [opposite, other_core(opposite), mine, own], GROUP - 2)

    def along_y(block, distance):
        return lax.ppermute(block, ("yl", "yh"), y_route(distance))

    half = NZ // 2
    parts = sweep(place, (2,), recv, src, GROUP - 2, False, begun, sizes=(half, half))
    by_left, by_right = along_y(parts[0], 1), along_y(parts[1], 3)
    ahead, behind = sweep(place, (1, 3), recv, src, GROUP - 2, False, begun, sizes=(NZ, NZ))
    ahead = along_y(ahead.at[:half].add(by_left), 1)
    behind = along_y(behind.at[half:].add(by_right), 3)
    (total,) = sweep(place, (0,), recv, src, GROUP, True)
    total = total + ahead + behind
    pieces = lax.all_to_all(total, "z", 0, 0, tiled=True)
    return direct + jnp.sum(pieces, axis=0)


def solution(mesh):
    fine = Mesh(mesh.devices.reshape(NX, NYL, NC, NYH, NZ), ("x", "yl", "c", "yh", "z"))
    blk, lane = ("x", "yl", "c"), ("yh", "z")
    both = blk + lane
    return jax.shard_map(
        shards,
        mesh=fine,
        in_specs=(
            P(None, both),
            P(None, both),
            P(None, both),
            P(None, both),
            P(both),
            P(both),
            P(both, None),
            P(both, None),
            P(blk, lane, None, None, None),
            P(blk, lane, None, None),
        ),
        out_specs=P(both, None),
        check_vma=False,
    )
```

```python
import functools

import jax
import jax.numpy as jnp
import numpy as np
from jax import lax
from jax.experimental import pallas as pl
from jax.experimental.pallas import tpu as pltpu
from jax.sharding import Mesh
from jax.sharding import PartitionSpec as P

NX, NYL, NC, NYH, NZ = 4, 2, 2, 2, 8
NY = NYL * NYH
BS = 128
SB = 8
CAP = 4
GROUP = NX * NC
NJ = NY * NZ
CENTRE = 3.0
TILE = 8
POS, NRM, AREA = 0, 3, 6
ROWS, DOT, SQA, SQB, ONE = 16, 8, 9, 10, 11
KF, KS, KD = 32, 32, 48
VMEM_LIMIT = 16 << 20
UNROLL, TAIL = 32, 8
FLUX = SB * BS
LISTS = FLUX + SB * TILE
LANES = NYH * NZ


def contraction_terms():
    pieces = [(i, j) for i in range(3) for j in range(3) if i + j < 4]

    def product(scale, rrow, srow):
        return [
            (scale, i * ROWS + rrow + a, j * ROWS + srow + a) for i, j in pieces for a in range(3)
        ]

    def from_recv(row, count):
        return [(1.0, i * ROWS + row, ONE) for i in range(count)]

    def from_src(row, count):
        return [(1.0, ONE, i * ROWS + row) for i in range(count)]

    facing = product(1.0, NRM, POS) + from_recv(DOT, 3)
    seen = product(1.0, POS, NRM) + from_src(DOT, 3)
    cross = product(-2.0, POS, POS)
    spread = (
        from_src(SQA, 2) + from_recv(SQA, 2) + cross + from_recv(SQB, 3) + from_src(SQB, 3)
    )
    return (KF, facing), (KS, seen), (KD, spread)


def selections(side):
    made = []
    for depth, terms in contraction_terms():
        groups = []
        for start in range(0, depth, 8):
            row = lax.broadcasted_iota(jnp.int32, (8, 3 * ROWS), 0)
            column = lax.broadcasted_iota(jnp.int32, (8, 3 * ROWS), 1)
            group = jnp.zeros((8, 3 * ROWS), jnp.float32)
            for at, term in enumerate(terms[start : start + 8]):
                value = term[0] if side == 0 else 1.0
                here = (row == at) & (column == term[1 + side])
                group = jnp.where(here, value, group)
            groups.append(group)
        made.append(jnp.concatenate(groups, axis=0).astype(jnp.bfloat16))
    return made


def split_pieces(tile):
    row = lax.broadcasted_iota(jnp.int32, tile.shape, 0)
    fixed = row < NRM
    coarse = jnp.where(fixed, jnp.round(tile * 32.0) * (1.0 / 32.0), tile)
    along = -(
        tile[NRM : NRM + 1] * tile[POS : POS + 1]
        + tile[NRM + 1 : NRM + 2] * tile[POS + 1 : POS + 2]
        + tile[NRM + 2 : NRM + 3] * tile[POS + 2 : POS + 3]
    )
    grid = [coarse[a : a + 1] for a in range(3)]
    fine = [tile[a : a + 1] - grid[a] for a in range(3)]
    square_a = grid[0] * grid[0] + grid[1] * grid[1] + grid[2] * grid[2]
    square_b = (
        fine[0] * (2.0 * grid[0] + fine[0])
        + fine[1] * (2.0 * grid[1] + fine[1])
        + fine[2] * (2.0 * grid[2] + fine[2])
    ) + tile[AREA : AREA + 1]
    derived = jnp.where(
        row == 0,
        along,
        jnp.where(
            row == 1, square_a, jnp.where(row == 2, square_b, jnp.where(row == 3, 1.0, 0.0))
        ),
    )
    values = jnp.concatenate([tile, derived], axis=0)
    high = jnp.concatenate([coarse, derived], axis=0).astype(jnp.bfloat16)
    rest = values - high.astype(jnp.float32)
    cut = lax.broadcasted_iota(jnp.int32, values.shape, 0) < NRM
    mid = jnp.where(cut, jnp.round(rest * 8192.0) * (1.0 / 8192.0), rest).astype(jnp.bfloat16)
    low = (rest - mid.astype(jnp.float32)).astype(jnp.bfloat16)
    return jnp.concatenate([high, mid, low], axis=0)


def dot(a, b):
    return jnp.dot(a, b, preferred_element_type=jnp.float32)


def direction(angles):
    polar, azimuth = angles[0:1], angles[1:2]
    across = jnp.sin(polar)
    return [across * jnp.cos(azimuth), across * jnp.sin(azimuth), jnp.cos(polar)]


def pack_kernel(*refs):
    given, (packed, recv_tile), held, arrival = refs[:9], refs[9:11], refs[11:20], refs[20]
    copies = [
        pltpu.make_async_copy(source, target, arrival.at[at])
        for at, (source, target) in enumerate(zip(given, held))
    ]
    for copy in copies:
        copy.start()
    for copy in copies:
        copy.wait()
    incident, pos, angles, area, keep, lists, counts, recv_pos, recv_angles = held
    packed[:FLUX, :] = incident[...].astype(jnp.float32)
    scale = keep[...] * area[...] * (1.0 / np.pi)
    rows = [pos[a : a + 1, :] - CENTRE for a in range(3)]
    rows += [component * scale for component in direction(angles[...])]
    rows += [area[...], jnp.zeros_like(scale)]
    tile = jnp.concatenate(rows, axis=0)
    slot = lax.broadcasted_iota(jnp.int32, (CAP, LANES), 0)
    for k in range(SB):
        packed[FLUX + k * TILE : FLUX + (k + 1) * TILE, :] = tile[:, k * BS : (k + 1) * BS]
    for k in range(GROUP):
        for yl in range(NYL):
            slab = ((k // NC) * NYL + yl) * NC + k % NC
            live = slot < counts[slab : slab + 1, :]
            marked = jnp.where(live, lists[slab], -1).astype(jnp.float32)
            rows = slice(LISTS + yl * CAP, LISTS + (yl + 1) * CAP)
            packed[rows, k * LANES : (k + 1) * LANES] = marked
    rows = [recv_pos[a : a + 1, :] - CENTRE for a in range(3)]
    rows += direction(recv_angles[...])
    rows += [jnp.zeros((2, BS), jnp.float32)]
    tile = jnp.concatenate(rows, axis=0)
    for j in range(NJ):
        recv_tile[j] = tile


def src_prep_kernel(count, *refs):
    packed = refs[:count]
    sf, ss, sd, em, lists = refs[count:]
    mats = selections(1)
    for d, ref in enumerate(packed):
        for k in range(SB):
            em[d * SB + k] = ref[k * BS : (k + 1) * BS, :].astype(jnp.bfloat16)
        tiles = [ref[FLUX + k * TILE : FLUX + (k + 1) * TILE, :] for k in range(SB)]
        q = split_pieces(jnp.concatenate(tiles, axis=1))
        lists[d] = ref[LISTS : LISTS + TILE, :].astype(jnp.int32)
        for m, out in zip(mats, (sf, ss, sd)):
            values = dot(m, q).astype(jnp.bfloat16)
            for k in range(SB):
                out[d * SB + k] = values[:, k * BS : (k + 1) * BS]
    null = count * SB
    em[null] = jnp.zeros((BS, BS), jnp.bfloat16)
    sf[null] = jnp.zeros((KF, BS), jnp.bfloat16)
    ss[null] = jnp.zeros((KS, BS), jnp.bfloat16)
    first_row = lax.broadcasted_iota(jnp.int32, (KD, BS), 0) == 0
    sd[null] = jnp.where(first_row, 1.0, 0.0).astype(jnp.bfloat16)


def recv_prep_kernel(tiles, rf, rs, rd):
    mats = selections(0)
    for j in range(NJ):
        q = split_pieces(tiles[j])
        for m, ref in zip(mats, (rf, rs, rd)):
            ref[j] = lax.dot_general(
                q, m, (((0,), (1,)), ((), ())), preferred_element_type=jnp.float32
            ).astype(jnp.bfloat16)


def sweep_kernel(count, distances, added, sizes, place, lists, rf, rs, rd, sf, ss, sd, em, *refs):
    before, outs = refs[:added], refs[added:-3]
    out, ids, owner = refs[-3:]
    blocks = len(distances) * NZ
    null = sf.shape[0] - 1
    slots = count * CAP // 2

    def block_of(j):
        ahead = distances[0]
        for at in range(1, len(distances)):
            ahead = jnp.where(j >= at * NZ, distances[at], ahead)
        target = (place[0] + ahead) & (NY - 1)
        return ((target & (NYL - 1)) * NYH + (target >> 1)) * NZ + (j & (NZ - 1))

    for j in range(blocks):
        start = jnp.zeros((BS, BS), jnp.float32)
        if added:
            start = before[0][(distances[j // NZ] - 1) * NZ + j % NZ]
        out[j] = start

    def one_block(j, n):
        block = block_of(j)
        row = (block >> 4) * CAP
        lane = place[1] * LANES + (block & (LANES - 1))
        for t in range(slots):
            owner[n // 2 + t] = j
        for d in range(count):
            used = []
            for c in range(CAP):
                value = lists[d, row + c, lane]
                ids[n + c] = d * SB + value
                used.append((value >= 0).astype(jnp.int32))
            n = n + ((used[0] + used[1]) + (used[2] + used[3]))
        ids[n] = null
        return n + n % 2

    n = lax.fori_loop(0, blocks, one_block, 0)
    for t in range(2 * TAIL):
        ids[n + t] = null
    for t in range(TAIL):
        owner[n // 2 + t] = 0

    def front(u):
        a, b = ids[2 * u], ids[2 * u + 1]
        j = block_of(owner[u])

        def pair(ref):
            return jnp.concatenate([ref[a], ref[b]], axis=1)

        facing = jnp.maximum(dot(rf[j], pair(sf)), 0.0)
        seen = jnp.maximum(dot(rs[j], pair(ss)), 0.0)
        spread = dot(rd[j], pair(sd))
        return (facing * seen / (spread * spread)).astype(jnp.bfloat16)

    def back(u, values):
        a, b = ids[2 * u], ids[2 * u + 1]
        j = owner[u]
        out[j] = out[j] + dot(values, jnp.concatenate([em[a], em[b]], axis=0))

    def run(first_unit, width, steps):
        def step(i, carry):
            units = [first_unit + i * width + r for r in range(width)]
            values = [front(u) for u in units]
            for u, value in zip(units, values):
                back(u, value)
            return carry

        lax.fori_loop(0, steps, step, 0)

    units = n // 2
    long = units // UNROLL
    run(0, UNROLL, long)
    run(long * UNROLL, TAIL, pl.cdiv(units - long * UNROLL, TAIL))
    at = 0
    for ref, size in zip(outs, sizes):
        ref[...] = out[at : at + size]
        at += size


VMEM_SPEC = pl.BlockSpec(memory_space=pltpu.VMEM)
SMEM_SPEC = pl.BlockSpec(memory_space=pltpu.SMEM)
BF16 = jnp.bfloat16
PARAMS = pltpu.CompilerParams(vmem_limit_bytes=VMEM_LIMIT)


def bf16_shape(*shape):
    return jax.ShapeDtypeStruct(shape, BF16)


def src_prep(packed):
    count = len(packed)
    rows = count * SB + 1
    return pl.pallas_call(
        functools.partial(src_prep_kernel, count),
        out_shape=[
            bf16_shape(rows, KF, BS),
            bf16_shape(rows, KS, BS),
            bf16_shape(rows, KD, BS),
            bf16_shape(rows, BS, BS),
            jax.ShapeDtypeStruct((count, 8, BS), jnp.int32),
        ],
        in_specs=[VMEM_SPEC] * count,
        out_specs=[VMEM_SPEC] * 5,
        name="src_prep",
        compiler_params=PARAMS,
        cost_estimate=pl.CostEstimate(flops=10**6, bytes_accessed=10**6, transcendentals=0),
    )(*packed)


def recv_prep(tiles):
    return pl.pallas_call(
        recv_prep_kernel,
        out_shape=[bf16_shape(NJ, BS, KF), bf16_shape(NJ, BS, KS), bf16_shape(NJ, BS, KD)],
        in_specs=[VMEM_SPEC],
        out_specs=[VMEM_SPEC] * 3,
        name="recv_prep",
        compiler_params=PARAMS,
        cost_estimate=pl.CostEstimate(flops=10**6, bytes_accessed=10**6, transcendentals=0),
    )(tiles)


def sweep(place, distances, recv, src, count, *before, sizes=None):
    *src, lists = src
    blocks = len(distances) * NZ
    sizes = sizes or (blocks,)
    return pl.pallas_call(
        functools.partial(sweep_kernel, count, distances, len(before), sizes),
        out_shape=[jax.ShapeDtypeStruct((size, BS, BS), jnp.float32) for size in sizes],
        in_specs=[SMEM_SPEC] * 2 + [VMEM_SPEC] * (7 + len(before)),
        out_specs=[VMEM_SPEC] * len(sizes),
        scratch_shapes=[
            pltpu.VMEM((blocks, BS, BS), jnp.float32),
            pltpu.SMEM((blocks * count * CAP + 4 * UNROLL,), jnp.int32),
            pltpu.SMEM((blocks * count * CAP // 2 + count * CAP + 2 * UNROLL,), jnp.int32),
        ],
        name="sweep",
        compiler_params=PARAMS,
        cost_estimate=pl.CostEstimate(flops=10**6, bytes_accessed=10**6, transcendentals=0),
    )(place, lists, *recv, *src, *before)


def pack(*operands):
    return pl.pallas_call(
        pack_kernel,
        out_shape=[
            jax.ShapeDtypeStruct((LISTS + TILE, BS), jnp.float32),
            jax.ShapeDtypeStruct((NJ, 8, BS), jnp.float32),
        ],
        in_specs=[pl.BlockSpec(memory_space=pltpu.HBM)] * 9,
        out_specs=[VMEM_SPEC] * 2,
        scratch_shapes=[pltpu.VMEM(array.shape, array.dtype) for array in operands]
        + [pltpu.SemaphoreType.DMA((9,))],
        name="pack",
        compiler_params=PARAMS,
        cost_estimate=pl.CostEstimate(flops=10**6, bytes_accessed=10**6, transcendentals=0),
    )(*[pltpu.with_memory_space_constraint(array, pltpu.HBM) for array in operands])


def y_route(distance):
    def linear(y):
        return (y % NYL) * NYH + y // NYL

    return [(linear(y), linear((y + distance) % NY)) for y in range(NY)]


def shards(
    recv_pos,
    recv_angles,
    src_pos,
    src_angles,
    src_area,
    reemission,
    incident,
    direct,
    visible_lists,
    visible_counts,
):
    mine, recv_tile = pack(
        incident,
        src_pos,
        src_angles,
        src_area.reshape(1, SB * BS),
        reemission.reshape(1, SB * BS),
        visible_lists[0, 0].transpose(0, 2, 1),
        visible_counts[0, 0],
        recv_pos,
        recv_angles,
    )

    def along_x(block, distance):
        return lax.ppermute(block, "x", [(i, (i + distance) % NX) for i in range(NX)])

    def other_core(block):
        return lax.ppermute(block, "c", [(0, 1), (1, 0)])

    my_y = lax.axis_index("yh") * NYL + lax.axis_index("yl")
    place = jnp.stack([my_y, lax.axis_index("x") * NC + lax.axis_index("c")]).astype(jnp.int32)
    far = [along_x(mine, distance) for distance in (1, 3, 2)]
    own = other_core(mine)

    tiles = lax.all_to_all(recv_tile, ("yl", "yh", "z"), 0, 0, tiled=True)

    own, tiles = lax.optimization_barrier((own, tiles))
    recv = recv_prep(tiles)
    (begun,) = sweep(place, (1, 2, 3), recv, src_prep([mine, own]), 2)
    *far, begun = lax.optimization_barrier((*far, begun))
    src = src_prep(far + [other_core(block) for block in far] + [mine, own])

    def along_y(block, distance):
        return lax.ppermute(block, ("yl", "yh"), y_route(distance))

    half = NZ // 2
    parts = sweep(place, (2,), recv, src, GROUP - 2, begun, sizes=(half, half))
    by_left, by_right = along_y(parts[0], 1), along_y(parts[1], 3)
    ahead, behind = sweep(place, (1, 3), recv, src, GROUP - 2, begun, sizes=(NZ, NZ))
    ahead = along_y(ahead.at[:half].add(by_left), 1)
    behind = along_y(behind.at[half:].add(by_right), 3)
    (total,) = sweep(place, (0,), recv, src, GROUP)
    total = total + ahead + behind
    pieces = lax.all_to_all(total, "z", 0, 0, tiled=True)
    return direct + jnp.sum(pieces, axis=0)


def solution(mesh):
    fine = Mesh(mesh.devices.reshape(NX, NYL, NC, NYH, NZ), ("x", "yl", "c", "yh", "z"))
    blk, lane = ("x", "yl", "c"), ("yh", "z")
    both = blk + lane
    return jax.shard_map(
        shards,
        mesh=fine,
        in_specs=(
            P(None, both),
            P(None, both),
            P(None, both),
            P(None, both),
            P(both),
            P(both),
            P(both, None),
            P(both, None),
            P(blk, lane, None, None, None),
            P(blk, lane, None, None),
        ),
        out_specs=P(both, None),
        check_vma=False,
    )
```

```python
import functools

import jax
import jax.numpy as jnp
import numpy as np
from jax import lax
from jax.experimental import pallas as pl
from jax.experimental.pallas import tpu as pltpu
from jax.sharding import Mesh
from jax.sharding import PartitionSpec as P

NX, NYL, NC, NYH, NZ = 4, 2, 2, 2, 8
NY = NYL * NYH
BS = 128
SB = 8
CAP = 4
GROUP = NX * NC
NJ = NY * NZ
CENTRE = 3.0
TILE = 8
POS, NRM, AREA = 0, 3, 6
ROWS, DOT, SQA, SQB, ONE = 16, 8, 9, 10, 11
KF, KS, KD = 32, 32, 48
VMEM_LIMIT = 16 << 20
UNROLL, TAIL = 32, 8
FLUX = SB * BS
LISTS = FLUX + SB * TILE
LANES = NYH * NZ


def contraction_terms():
    pieces = [(i, j) for i in range(3) for j in range(3) if i + j < 4]

    def product(scale, rrow, srow):
        return [
            (scale, i * ROWS + rrow + a, j * ROWS + srow + a) for i, j in pieces for a in range(3)
        ]

    def from_recv(row, count):
        return [(1.0, i * ROWS + row, ONE) for i in range(count)]

    def from_src(row, count):
        return [(1.0, ONE, i * ROWS + row) for i in range(count)]

    facing = product(1.0, NRM, POS) + from_recv(DOT, 3)
    seen = product(1.0, POS, NRM) + from_src(DOT, 3)
    cross = product(-2.0, POS, POS)
    spread = (
        from_src(SQA, 2) + from_recv(SQA, 2) + cross + from_recv(SQB, 3) + from_src(SQB, 3)
    )
    return (KF, facing), (KS, seen), (KD, spread)


def selections(side):
    made = []
    for depth, terms in contraction_terms():
        groups = []
        for start in range(0, depth, 8):
            row = lax.broadcasted_iota(jnp.int32, (8, 3 * ROWS), 0)
            column = lax.broadcasted_iota(jnp.int32, (8, 3 * ROWS), 1)
            group = jnp.zeros((8, 3 * ROWS), jnp.float32)
            for at, term in enumerate(terms[start : start + 8]):
                value = term[0] if side == 0 else 1.0
                here = (row == at) & (column == term[1 + side])
                group = jnp.where(here, value, group)
            groups.append(group)
        made.append(jnp.concatenate(groups, axis=0).astype(jnp.bfloat16))
    return made


def split_pieces(tile):
    row = lax.broadcasted_iota(jnp.int32, tile.shape, 0)
    fixed = row < NRM
    coarse = jnp.where(fixed, jnp.round(tile * 32.0) * (1.0 / 32.0), tile)
    along = -(
        tile[NRM : NRM + 1] * tile[POS : POS + 1]
        + tile[NRM + 1 : NRM + 2] * tile[POS + 1 : POS + 2]
        + tile[NRM + 2 : NRM + 3] * tile[POS + 2 : POS + 3]
    )
    grid = [coarse[a : a + 1] for a in range(3)]
    fine = [tile[a : a + 1] - grid[a] for a in range(3)]
    square_a = grid[0] * grid[0] + grid[1] * grid[1] + grid[2] * grid[2]
    square_b = (
        fine[0] * (2.0 * grid[0] + fine[0])
        + fine[1] * (2.0 * grid[1] + fine[1])
        + fine[2] * (2.0 * grid[2] + fine[2])
    ) + tile[AREA : AREA + 1]
    derived = jnp.where(
        row == 0,
        along,
        jnp.where(
            row == 1, square_a, jnp.where(row == 2, square_b, jnp.where(row == 3, 1.0, 0.0))
        ),
    )
    values = jnp.concatenate([tile, derived], axis=0)
    high = jnp.concatenate([coarse, derived], axis=0).astype(jnp.bfloat16)
    rest = values - high.astype(jnp.float32)
    cut = lax.broadcasted_iota(jnp.int32, values.shape, 0) < NRM
    mid = jnp.where(cut, jnp.round(rest * 8192.0) * (1.0 / 8192.0), rest).astype(jnp.bfloat16)
    low = (rest - mid.astype(jnp.float32)).astype(jnp.bfloat16)
    return jnp.concatenate([high, mid, low], axis=0)


def dot(a, b):
    return jnp.dot(a, b, preferred_element_type=jnp.float32)


def direction(angles):
    polar, azimuth = angles[0:1], angles[1:2]
    across = jnp.sin(polar)
    return [across * jnp.cos(azimuth), across * jnp.sin(azimuth), jnp.cos(polar)]


def pack_kernel(*refs):
    given, (packed, recv_tile), held, arrival = refs[:9], refs[9:11], refs[11:20], refs[20]
    copies = [
        pltpu.make_async_copy(source, target, arrival.at[at])
        for at, (source, target) in enumerate(zip(given, held))
    ]
    for copy in copies:
        copy.start()
    for copy in copies:
        copy.wait()
    incident, pos, angles, area, keep, lists, counts, recv_pos, recv_angles = held
    packed[:FLUX, :] = incident[...].astype(jnp.float32)
    scale = keep[...] * area[...] * (1.0 / np.pi)
    rows = [pos[a : a + 1, :] - CENTRE for a in range(3)]
    rows += [component * scale for component in direction(angles[...])]
    rows += [area[...], jnp.zeros_like(scale)]
    tile = jnp.concatenate(rows, axis=0)
    slot = lax.broadcasted_iota(jnp.int32, (CAP, LANES), 0)
    for k in range(SB):
        packed[FLUX + k * TILE : FLUX + (k + 1) * TILE, :] = tile[:, k * BS : (k + 1) * BS]
    for k in range(GROUP):
        for yl in range(NYL):
            slab = ((k // NC) * NYL + yl) * NC + k % NC
            live = slot < counts[slab : slab + 1, :]
            marked = jnp.where(live, lists[slab], -1).astype(jnp.float32)
            rows = slice(LISTS + yl * CAP, LISTS + (yl + 1) * CAP)
            packed[rows, k * LANES : (k + 1) * LANES] = marked
    rows = [recv_pos[a : a + 1, :] - CENTRE for a in range(3)]
    rows += direction(recv_angles[...])
    rows += [jnp.zeros((2, BS), jnp.float32)]
    tile = jnp.concatenate(rows, axis=0)
    for j in range(NJ):
        recv_tile[j] = tile


def src_prep_kernel(count, place, *refs):
    packed = refs[:count]
    sf, ss, sd, em, lists = refs[count:]
    mats = selections(1)
    for d, ref in enumerate(packed):
        for k in range(SB):
            em[d * SB + k] = ref[k * BS : (k + 1) * BS, :].astype(jnp.bfloat16)
        tiles = [ref[FLUX + k * TILE : FLUX + (k + 1) * TILE, :] for k in range(SB)]
        q = split_pieces(jnp.concatenate(tiles, axis=1))
        tile = ref[LISTS : LISTS + TILE, :]
        tile = pltpu.roll(tile, 0, 1, stride=LANES, stride_axis=0)
        tile = pltpu.roll(tile, (GROUP - place[1]) * LANES, 1)
        row = lax.broadcasted_iota(jnp.int32, tile.shape, 0)
        lane = lax.broadcasted_iota(jnp.int32, tile.shape, 1)
        side = jnp.sum(jnp.where((lane >> 4) == row, tile, 0.0), axis=0, keepdims=True)
        lists[d : d + 1, :] = side.astype(jnp.int32)
        for m, out in zip(mats, (sf, ss, sd)):
            values = dot(m, q).astype(jnp.bfloat16)
            for k in range(SB):
                out[d * SB + k] = values[:, k * BS : (k + 1) * BS]
    null = count * SB
    em[null] = jnp.zeros((BS, BS), jnp.bfloat16)
    sf[null] = jnp.zeros((KF, BS), jnp.bfloat16)
    ss[null] = jnp.zeros((KS, BS), jnp.bfloat16)
    first_row = lax.broadcasted_iota(jnp.int32, (KD, BS), 0) == 0
    sd[null] = jnp.where(first_row, 1.0, 0.0).astype(jnp.bfloat16)


def recv_prep_kernel(tiles, rf, rs, rd):
    mats = selections(0)
    for j in range(NJ):
        q = split_pieces(tiles[j])
        for m, ref in zip(mats, (rf, rs, rd)):
            ref[j] = lax.dot_general(
                q, m, (((0,), (1,)), ((), ())), preferred_element_type=jnp.float32
            ).astype(jnp.bfloat16)


def sweep_kernel(count, distances, added, sizes, place, lists, rf, rs, rd, sf, ss, sd, em, *refs):
    before, outs = refs[:added], refs[added:-3]
    out, ids, owner = refs[-3:]
    if len(sizes) == 1:
        out = outs[0]
    blocks = len(distances) * NZ
    null = sf.shape[0] - 1
    slots = count * CAP // 2

    def block_of(j):
        ahead = distances[0]
        for at in range(1, len(distances)):
            ahead = jnp.where(j >= at * NZ, distances[at], ahead)
        target = (place[0] + ahead) & (NY - 1)
        return ((target & (NYL - 1)) * NYH + (target >> 1)) * NZ + (j & (NZ - 1))

    for j in range(blocks):
        start = jnp.zeros((BS, BS), jnp.float32)
        if added:
            start = before[0][(distances[j // NZ] - 1) * NZ + j % NZ]
        out[j] = start

    def one_block(j, n):
        block = block_of(j)
        lane = (block >> 4) * CAP * LANES + (block & (LANES - 1))
        for t in range(slots):
            owner[n // 2 + t] = j
        for d in range(count):
            used = []
            for c in range(CAP):
                value = lists[d, lane + c * LANES]
                ids[n + c] = d * SB + value
                used.append((value >= 0).astype(jnp.int32))
            n = n + ((used[0] + used[1]) + (used[2] + used[3]))
        ids[n] = null
        return n + n % 2

    n = lax.fori_loop(0, blocks, one_block, 0)
    for t in range(2 * TAIL):
        ids[n + t] = null
    for t in range(TAIL):
        owner[n // 2 + t] = 0

    def front(u):
        a, b = ids[2 * u], ids[2 * u + 1]
        j = block_of(owner[u])

        def pair(ref):
            return jnp.concatenate([ref[a], ref[b]], axis=1)

        facing = jnp.maximum(dot(rf[j], pair(sf)), 0.0)
        seen = jnp.maximum(dot(rs[j], pair(ss)), 0.0)
        spread = dot(rd[j], pair(sd))
        return (facing * seen / (spread * spread)).astype(jnp.bfloat16)

    def back(u, values):
        a, b = ids[2 * u], ids[2 * u + 1]
        j = owner[u]
        out[j] = out[j] + dot(values, jnp.concatenate([em[a], em[b]], axis=0))

    def run(first_unit, width, steps):
        def step(i, carry):
            units = [first_unit + i * width + r for r in range(width)]
            values = [front(u) for u in units]
            for u, value in zip(units, values):
                back(u, value)
            return carry

        lax.fori_loop(0, steps, step, 0)

    units = n // 2
    long = units // UNROLL
    run(0, UNROLL, long)
    run(long * UNROLL, TAIL, pl.cdiv(units - long * UNROLL, TAIL))
    if len(sizes) > 1:
        at = 0
        for ref, size in zip(outs, sizes):
            ref[...] = out[at : at + size]
            at += size


VMEM_SPEC = pl.BlockSpec(memory_space=pltpu.VMEM)
SMEM_SPEC = pl.BlockSpec(memory_space=pltpu.SMEM)
BF16 = jnp.bfloat16
PARAMS = pltpu.CompilerParams(vmem_limit_bytes=VMEM_LIMIT)


def bf16_shape(*shape):
    return jax.ShapeDtypeStruct(shape, BF16)


def src_prep(place, packed):
    count = len(packed)
    rows = count * SB + 1
    return pl.pallas_call(
        functools.partial(src_prep_kernel, count),
        out_shape=[
            bf16_shape(rows, KF, BS),
            bf16_shape(rows, KS, BS),
            bf16_shape(rows, KD, BS),
            bf16_shape(rows, BS, BS),
            jax.ShapeDtypeStruct((count, BS), jnp.int32),
        ],
        in_specs=[SMEM_SPEC] + [VMEM_SPEC] * count,
        out_specs=[VMEM_SPEC] * 5,
        name="src_prep",
        compiler_params=PARAMS,
        cost_estimate=pl.CostEstimate(flops=10**6, bytes_accessed=10**6, transcendentals=0),
    )(place, *packed)


def recv_prep(tiles):
    return pl.pallas_call(
        recv_prep_kernel,
        out_shape=[bf16_shape(NJ, BS, KF), bf16_shape(NJ, BS, KS), bf16_shape(NJ, BS, KD)],
        in_specs=[VMEM_SPEC],
        out_specs=[VMEM_SPEC] * 3,
        name="recv_prep",
        compiler_params=PARAMS,
        cost_estimate=pl.CostEstimate(flops=10**6, bytes_accessed=10**6, transcendentals=0),
    )(tiles)


def sweep(place, distances, recv, src, count, *before, sizes=None):
    *src, lists = src
    blocks = len(distances) * NZ
    sizes = sizes or (blocks,)
    return pl.pallas_call(
        functools.partial(sweep_kernel, count, distances, len(before), sizes),
        out_shape=[jax.ShapeDtypeStruct((size, BS, BS), jnp.float32) for size in sizes],
        in_specs=[SMEM_SPEC] * 2 + [VMEM_SPEC] * (7 + len(before)),
        out_specs=[VMEM_SPEC] * len(sizes),
        scratch_shapes=[
            pltpu.VMEM((blocks if len(sizes) > 1 else 1, BS, BS), jnp.float32),
            pltpu.SMEM((blocks * count * CAP + 4 * UNROLL,), jnp.int32),
            pltpu.SMEM((blocks * count * CAP // 2 + count * CAP + 2 * UNROLL,), jnp.int32),
        ],
        name="sweep",
        compiler_params=PARAMS,
        cost_estimate=pl.CostEstimate(flops=10**6, bytes_accessed=10**6, transcendentals=0),
    )(place, lists, *recv, *src, *before)


def pack(*operands):
    return pl.pallas_call(
        pack_kernel,
        out_shape=[
            jax.ShapeDtypeStruct((LISTS + TILE, BS), jnp.float32),
            jax.ShapeDtypeStruct((NJ, 8, BS), jnp.float32),
        ],
        in_specs=[pl.BlockSpec(memory_space=pltpu.HBM)] * 9,
        out_specs=[VMEM_SPEC] * 2,
        scratch_shapes=[pltpu.VMEM(array.shape, array.dtype) for array in operands]
        + [pltpu.SemaphoreType.DMA((9,))],
        name="pack",
        compiler_params=PARAMS,
        cost_estimate=pl.CostEstimate(flops=10**6, bytes_accessed=10**6, transcendentals=0),
    )(*[pltpu.with_memory_space_constraint(array, pltpu.HBM) for array in operands])


def y_route(distance):
    def linear(y):
        return (y % NYL) * NYH + y // NYL

    return [(linear(y), linear((y + distance) % NY)) for y in range(NY)]


def shards(
    recv_pos,
    recv_angles,
    src_pos,
    src_angles,
    src_area,
    reemission,
    incident,
    direct,
    visible_lists,
    visible_counts,
):
    mine, recv_tile = pack(
        incident,
        src_pos,
        src_angles,
        src_area.reshape(1, SB * BS),
        reemission.reshape(1, SB * BS),
        visible_lists[0, 0].transpose(0, 2, 1),
        visible_counts[0, 0],
        recv_pos,
        recv_angles,
    )

    def along_x(block, distance):
        return lax.ppermute(block, "x", [(i, (i + distance) % NX) for i in range(NX)])

    def other_core(block):
        return lax.ppermute(block, "c", [(0, 1), (1, 0)])

    my_y = lax.axis_index("yh") * NYL + lax.axis_index("yl")
    place = jnp.stack([my_y, lax.axis_index("x") * NC + lax.axis_index("c")]).astype(jnp.int32)
    far = [along_x(mine, distance) for distance in (1, 3, 2)]
    own = other_core(mine)

    tiles = lax.all_to_all(recv_tile, ("yl", "yh", "z"), 0, 0, tiled=True)

    own, tiles = lax.optimization_barrier((own, tiles))
    recv = recv_prep(tiles)
    (begun,) = sweep(place, (1, 2, 3), recv, src_prep(place, [mine, own]), 2)
    *far, begun = lax.optimization_barrier((*far, begun))
    src = src_prep(place, far + [other_core(block) for block in far] + [mine, own])

    def along_y(block, distance):
        return lax.ppermute(block, ("yl", "yh"), y_route(distance))

    half = NZ // 2
    parts = sweep(place, (2,), recv, src, GROUP - 2, begun, sizes=(half, half))
    by_left, by_right = along_y(parts[0], 1), along_y(parts[1], 3)
    ahead, behind = sweep(place, (1, 3), recv, src, GROUP - 2, begun, sizes=(NZ, NZ))
    ahead = along_y(ahead.at[:half].add(by_left), 1)
    behind = along_y(behind.at[half:].add(by_right), 3)
    (total,) = sweep(place, (0,), recv, src, GROUP)
    total = total + ahead + behind
    pieces = lax.all_to_all(total, "z", 0, 0, tiled=True)
    return direct + jnp.sum(pieces, axis=0)


def solution(mesh):
    fine = Mesh(mesh.devices.reshape(NX, NYL, NC, NYH, NZ), ("x", "yl", "c", "yh", "z"))
    blk, lane = ("x", "yl", "c"), ("yh", "z")
    both = blk + lane
    return jax.shard_map(
        shards,
        mesh=fine,
        in_specs=(
            P(None, both),
            P(None, both),
            P(None, both),
            P(None, both),
            P(both),
            P(both),
            P(both, None),
            P(both, None),
            P(blk, lane, None, None, None),
            P(blk, lane, None, None),
        ),
        out_specs=P(both, None),
        check_vma=False,
    )
```

```python
import functools

import jax
import jax.numpy as jnp
import numpy as np
from jax import lax
from jax.experimental import pallas as pl
from jax.experimental.pallas import tpu as pltpu
from jax.sharding import Mesh
from jax.sharding import PartitionSpec as P

NX, NYL, NC, NYH, NZ = 4, 2, 2, 2, 8
NY = NYL * NYH
BS = 128
SB = 8
CAP = 4
GROUP = NX * NC
NJ = NY * NZ
CENTRE = 3.0
TILE = 8
POS, NRM, AREA = 0, 3, 6
ROWS, DOT, SQA, SQB, ONE = 16, 8, 9, 10, 11
KF, KS, KD = 32, 32, 48
VMEM_LIMIT = 16 << 20
UNROLL, TAIL = 32, 8
FLUX = SB * BS
LISTS = FLUX + SB * TILE
LANES = NYH * NZ


def contraction_terms():
    pieces = [(i, j) for i in range(3) for j in range(3) if i + j < 4]

    def product(scale, rrow, srow):
        return [
            (scale, i * ROWS + rrow + a, j * ROWS + srow + a) for i, j in pieces for a in range(3)
        ]

    def from_recv(row, count):
        return [(1.0, i * ROWS + row, ONE) for i in range(count)]

    def from_src(row, count):
        return [(1.0, ONE, i * ROWS + row) for i in range(count)]

    facing = product(1.0, NRM, POS) + from_recv(DOT, 3)
    seen = product(1.0, POS, NRM) + from_src(DOT, 3)
    cross = product(-2.0, POS, POS)
    spread = (
        from_src(SQA, 2) + from_recv(SQA, 2) + cross + from_recv(SQB, 3) + from_src(SQB, 3)
    )
    return (KF, facing), (KS, seen), (KD, spread)


def selections(side):
    made = []
    for depth, terms in contraction_terms():
        groups = []
        for start in range(0, depth, 8):
            row = lax.broadcasted_iota(jnp.int32, (8, 3 * ROWS), 0)
            column = lax.broadcasted_iota(jnp.int32, (8, 3 * ROWS), 1)
            group = jnp.zeros((8, 3 * ROWS), jnp.float32)
            for at, term in enumerate(terms[start : start + 8]):
                value = term[0] if side == 0 else 1.0
                here = (row == at) & (column == term[1 + side])
                group = jnp.where(here, value, group)
            groups.append(group)
        made.append(jnp.concatenate(groups, axis=0).astype(jnp.bfloat16))
    return made


def split_pieces(tile):
    row = lax.broadcasted_iota(jnp.int32, tile.shape, 0)
    fixed = row < NRM
    coarse = jnp.where(fixed, jnp.round(tile * 32.0) * (1.0 / 32.0), tile)
    along = -(
        tile[NRM : NRM + 1] * tile[POS : POS + 1]
        + tile[NRM + 1 : NRM + 2] * tile[POS + 1 : POS + 2]
        + tile[NRM + 2 : NRM + 3] * tile[POS + 2 : POS + 3]
    )
    grid = [coarse[a : a + 1] for a in range(3)]
    fine = [tile[a : a + 1] - grid[a] for a in range(3)]
    square_a = grid[0] * grid[0] + grid[1] * grid[1] + grid[2] * grid[2]
    square_b = (
        fine[0] * (2.0 * grid[0] + fine[0])
        + fine[1] * (2.0 * grid[1] + fine[1])
        + fine[2] * (2.0 * grid[2] + fine[2])
    ) + tile[AREA : AREA + 1]
    derived = jnp.where(
        row == 0,
        along,
        jnp.where(
            row == 1, square_a, jnp.where(row == 2, square_b, jnp.where(row == 3, 1.0, 0.0))
        ),
    )
    values = jnp.concatenate([tile, derived], axis=0)
    high = jnp.concatenate([coarse, derived], axis=0).astype(jnp.bfloat16)
    rest = values - high.astype(jnp.float32)
    cut = lax.broadcasted_iota(jnp.int32, values.shape, 0) < NRM
    mid = jnp.where(cut, jnp.round(rest * 8192.0) * (1.0 / 8192.0), rest).astype(jnp.bfloat16)
    low = (rest - mid.astype(jnp.float32)).astype(jnp.bfloat16)
    return jnp.concatenate([high, mid, low], axis=0)


def dot(a, b):
    return jnp.dot(a, b, preferred_element_type=jnp.float32)


def direction(angles):
    polar, azimuth = angles[0:1], angles[1:2]
    across = jnp.sin(polar)
    return [across * jnp.cos(azimuth), across * jnp.sin(azimuth), jnp.cos(polar)]


def pack_kernel(*refs):
    given, (packed, recv_tile), held, arrival = refs[:9], refs[9:11], refs[11:20], refs[20]
    copies = [
        pltpu.make_async_copy(source, target, arrival.at[at])
        for at, (source, target) in enumerate(zip(given, held))
    ]
    for copy in copies:
        copy.start()
    for copy in copies:
        copy.wait()
    incident, pos, angles, area, keep, lists, counts, recv_pos, recv_angles = held
    packed[:FLUX, :] = incident[...].astype(jnp.float32)
    scale = keep[...] * area[...] * (1.0 / np.pi)
    rows = [pos[a : a + 1, :] - CENTRE for a in range(3)]
    rows += [component * scale for component in direction(angles[...])]
    rows += [area[...], jnp.zeros_like(scale)]
    tile = jnp.concatenate(rows, axis=0)
    slot = lax.broadcasted_iota(jnp.int32, (CAP, LANES), 0)
    for k in range(SB):
        packed[FLUX + k * TILE : FLUX + (k + 1) * TILE, :] = tile[:, k * BS : (k + 1) * BS]
    for k in range(GROUP):
        for yl in range(NYL):
            slab = ((k // NC) * NYL + yl) * NC + k % NC
            live = slot < counts[slab : slab + 1, :]
            marked = jnp.where(live, lists[slab], -1).astype(jnp.float32)
            for c in range(CAP):
                at = (yl * CAP + c) * LANES
                packed[LISTS + k : LISTS + k + 1, at : at + LANES] = marked[c : c + 1, :]
    rows = [recv_pos[a : a + 1, :] - CENTRE for a in range(3)]
    rows += direction(recv_angles[...])
    rows += [jnp.zeros((2, BS), jnp.float32)]
    tile = jnp.concatenate(rows, axis=0)
    for j in range(NJ):
        recv_tile[j] = tile


def src_prep_kernel(count, place, *refs):
    packed = refs[:count]
    sf, ss, sd, em, lists = refs[count:]
    mats = selections(1)
    for d, ref in enumerate(packed):
        for k in range(SB):
            em[d * SB + k] = ref[k * BS : (k + 1) * BS, :].astype(jnp.bfloat16)
        tiles = [ref[FLUX + k * TILE : FLUX + (k + 1) * TILE, :] for k in range(SB)]
        q = split_pieces(jnp.concatenate(tiles, axis=1))
        lists[d : d + 1, :] = ref[pl.ds(LISTS + place[1], 1), :].astype(jnp.int32)
        for m, out in zip(mats, (sf, ss, sd)):
            values = dot(m, q).astype(jnp.bfloat16)
            for k in range(SB):
                out[d * SB + k] = values[:, k * BS : (k + 1) * BS]
    null = count * SB
    em[null] = jnp.zeros((BS, BS), jnp.bfloat16)
    sf[null] = jnp.zeros((KF, BS), jnp.bfloat16)
    ss[null] = jnp.zeros((KS, BS), jnp.bfloat16)
    first_row = lax.broadcasted_iota(jnp.int32, (KD, BS), 0) == 0
    sd[null] = jnp.where(first_row, 1.0, 0.0).astype(jnp.bfloat16)


def recv_prep_kernel(tiles, rf, rs, rd):
    mats = selections(0)
    for j in range(NJ):
        q = split_pieces(tiles[j])
        for m, ref in zip(mats, (rf, rs, rd)):
            ref[j] = lax.dot_general(
                q, m, (((0,), (1,)), ((), ())), preferred_element_type=jnp.float32
            ).astype(jnp.bfloat16)


def sweep_kernel(count, distances, added, sizes, place, lists, rf, rs, rd, sf, ss, sd, em, *refs):
    before, outs = refs[:added], refs[added:-3]
    out, ids, owner = refs[-3:]
    if len(sizes) == 1:
        out = outs[0]
    blocks = len(distances) * NZ
    null = sf.shape[0] - 1
    slots = count * CAP // 2

    def block_of(j):
        ahead = distances[0]
        for at in range(1, len(distances)):
            ahead = jnp.where(j >= at * NZ, distances[at], ahead)
        target = (place[0] + ahead) & (NY - 1)
        return ((target & (NYL - 1)) * NYH + (target >> 1)) * NZ + (j & (NZ - 1))

    for j in range(blocks):
        start = jnp.zeros((BS, BS), jnp.float32)
        if added:
            start = before[0][(distances[j // NZ] - 1) * NZ + j % NZ]
        out[j] = start

    def one_block(j, n):
        block = block_of(j)
        lane = (block >> 4) * CAP * LANES + (block & (LANES - 1))
        for t in range(slots):
            owner[n // 2 + t] = j
        for d in range(count):
            used = []
            for c in range(CAP):
                value = lists[d, lane + c * LANES]
                ids[n + c] = d * SB + value
                used.append((value >= 0).astype(jnp.int32))
            n = n + ((used[0] + used[1]) + (used[2] + used[3]))
        ids[n] = null
        return n + n % 2

    n = lax.fori_loop(0, blocks, one_block, 0)
    for t in range(2 * TAIL):
        ids[n + t] = null
    for t in range(TAIL):
        owner[n // 2 + t] = 0

    def front(u):
        a, b = ids[2 * u], ids[2 * u + 1]
        j = block_of(owner[u])

        def pair(ref):
            return jnp.concatenate([ref[a], ref[b]], axis=1)

        facing = jnp.maximum(dot(rf[j], pair(sf)), 0.0)
        seen = jnp.maximum(dot(rs[j], pair(ss)), 0.0)
        spread = dot(rd[j], pair(sd))
        return (facing * seen / (spread * spread)).astype(jnp.bfloat16)

    def back(u, values):
        a, b = ids[2 * u], ids[2 * u + 1]
        j = owner[u]
        out[j] = out[j] + dot(values, jnp.concatenate([em[a], em[b]], axis=0))

    def run(first_unit, width, steps):
        def step(i, carry):
            units = [first_unit + i * width + r for r in range(width)]
            values = [front(u) for u in units]
            for u, value in zip(units, values):
                back(u, value)
            return carry

        lax.fori_loop(0, steps, step, 0)

    units = n // 2
    long = units // UNROLL
    run(0, UNROLL, long)
    run(long * UNROLL, TAIL, pl.cdiv(units - long * UNROLL, TAIL))
    if len(sizes) > 1:
        at = 0
        for ref, size in zip(outs, sizes):
            ref[...] = out[at : at + size]
            at += size


VMEM_SPEC = pl.BlockSpec(memory_space=pltpu.VMEM)
SMEM_SPEC = pl.BlockSpec(memory_space=pltpu.SMEM)
BF16 = jnp.bfloat16
PARAMS = pltpu.CompilerParams(vmem_limit_bytes=VMEM_LIMIT)


def bf16_shape(*shape):
    return jax.ShapeDtypeStruct(shape, BF16)


def src_prep(place, packed):
    count = len(packed)
    rows = count * SB + 1
    return pl.pallas_call(
        functools.partial(src_prep_kernel, count),
        out_shape=[
            bf16_shape(rows, KF, BS),
            bf16_shape(rows, KS, BS),
            bf16_shape(rows, KD, BS),
            bf16_shape(rows, BS, BS),
            jax.ShapeDtypeStruct((count, BS), jnp.int32),
        ],
        in_specs=[SMEM_SPEC] + [VMEM_SPEC] * count,
        out_specs=[VMEM_SPEC] * 5,
        name="src_prep",
        compiler_params=PARAMS,
        cost_estimate=pl.CostEstimate(flops=10**6, bytes_accessed=10**6, transcendentals=0),
    )(place, *packed)


def recv_prep(tiles):
    return pl.pallas_call(
        recv_prep_kernel,
        out_shape=[bf16_shape(NJ, BS, KF), bf16_shape(NJ, BS, KS), bf16_shape(NJ, BS, KD)],
        in_specs=[VMEM_SPEC],
        out_specs=[VMEM_SPEC] * 3,
        name="recv_prep",
        compiler_params=PARAMS,
        cost_estimate=pl.CostEstimate(flops=10**6, bytes_accessed=10**6, transcendentals=0),
    )(tiles)


def sweep(place, distances, recv, src, count, *before, sizes=None):
    *src, lists = src
    blocks = len(distances) * NZ
    sizes = sizes or (blocks,)
    return pl.pallas_call(
        functools.partial(sweep_kernel, count, distances, len(before), sizes),
        out_shape=[jax.ShapeDtypeStruct((size, BS, BS), jnp.float32) for size in sizes],
        in_specs=[SMEM_SPEC] * 2 + [VMEM_SPEC] * (7 + len(before)),
        out_specs=[VMEM_SPEC] * len(sizes),
        scratch_shapes=[
            pltpu.VMEM((blocks if len(sizes) > 1 else 1, BS, BS), jnp.float32),
            pltpu.SMEM((blocks * count * CAP + 4 * UNROLL,), jnp.int32),
            pltpu.SMEM((blocks * count * CAP // 2 + count * CAP + 2 * UNROLL,), jnp.int32),
        ],
        name="sweep",
        compiler_params=PARAMS,
        cost_estimate=pl.CostEstimate(flops=10**6, bytes_accessed=10**6, transcendentals=0),
    )(place, lists, *recv, *src, *before)


def pack(*operands):
    return pl.pallas_call(
        pack_kernel,
        out_shape=[
            jax.ShapeDtypeStruct((LISTS + TILE, BS), jnp.float32),
            jax.ShapeDtypeStruct((NJ, 8, BS), jnp.float32),
        ],
        in_specs=[pl.BlockSpec(memory_space=pltpu.HBM)] * 9,
        out_specs=[VMEM_SPEC] * 2,
        scratch_shapes=[pltpu.VMEM(array.shape, array.dtype) for array in operands]
        + [pltpu.SemaphoreType.DMA((9,))],
        name="pack",
        compiler_params=PARAMS,
        cost_estimate=pl.CostEstimate(flops=10**6, bytes_accessed=10**6, transcendentals=0),
    )(*[pltpu.with_memory_space_constraint(array, pltpu.HBM) for array in operands])


def y_route(distance):
    def linear(y):
        return (y % NYL) * NYH + y // NYL

    return [(linear(y), linear((y + distance) % NY)) for y in range(NY)]


def shards(
    recv_pos,
    recv_angles,
    src_pos,
    src_angles,
    src_area,
    reemission,
    incident,
    direct,
    visible_lists,
    visible_counts,
):
    mine, recv_tile = pack(
        incident,
        src_pos,
        src_angles,
        src_area.reshape(1, SB * BS),
        reemission.reshape(1, SB * BS),
        visible_lists[0, 0].transpose(0, 2, 1),
        visible_counts[0, 0],
        recv_pos,
        recv_angles,
    )

    def along_x(block, distance):
        return lax.ppermute(block, "x", [(i, (i + distance) % NX) for i in range(NX)])

    def other_core(block):
        return lax.ppermute(block, "c", [(0, 1), (1, 0)])

    my_y = lax.axis_index("yh") * NYL + lax.axis_index("yl")
    place = jnp.stack([my_y, lax.axis_index("x") * NC + lax.axis_index("c")]).astype(jnp.int32)
    far = [along_x(mine, distance) for distance in (1, 3, 2)]
    own = other_core(mine)

    tiles = lax.all_to_all(recv_tile, ("yl", "yh", "z"), 0, 0, tiled=True)

    own, tiles = lax.optimization_barrier((own, tiles))
    recv = recv_prep(tiles)
    (begun,) = sweep(place, (1, 2, 3), recv, src_prep(place, [mine, own]), 2)
    *far, begun = lax.optimization_barrier((*far, begun))
    src = src_prep(place, far + [other_core(block) for block in far] + [mine, own])

    def along_y(block, distance):
        return lax.ppermute(block, ("yl", "yh"), y_route(distance))

    half = NZ // 2
    parts = sweep(place, (2,), recv, src, GROUP - 2, begun, sizes=(half, half))
    by_left, by_right = along_y(parts[0], 1), along_y(parts[1], 3)
    ahead, behind = sweep(place, (1, 3), recv, src, GROUP - 2, begun, sizes=(NZ, NZ))
    ahead = along_y(ahead.at[:half].add(by_left), 1)
    behind = along_y(behind.at[half:].add(by_right), 3)
    (total,) = sweep(place, (0,), recv, src, GROUP)
    total = total + ahead + behind
    pieces = lax.all_to_all(total, "z", 0, 0, tiled=True)
    return direct + jnp.sum(pieces, axis=0)


def solution(mesh):
    fine = Mesh(mesh.devices.reshape(NX, NYL, NC, NYH, NZ), ("x", "yl", "c", "yh", "z"))
    blk, lane = ("x", "yl", "c"), ("yh", "z")
    both = blk + lane
    return jax.shard_map(
        shards,
        mesh=fine,
        in_specs=(
            P(None, both),
            P(None, both),
            P(None, both),
            P(None, both),
            P(both),
            P(both),
            P(both, None),
            P(both, None),
            P(blk, lane, None, None, None),
            P(blk, lane, None, None),
        ),
        out_specs=P(both, None),
        check_vma=False,
    )
```

```python
import functools

import jax
import jax.numpy as jnp
import numpy as np
from jax import lax
from jax.experimental import pallas as pl
from jax.experimental.pallas import tpu as pltpu
from jax.sharding import Mesh
from jax.sharding import PartitionSpec as P

NX, NYL, NC, NYH, NZ = 4, 2, 2, 2, 8
NY = NYL * NYH
BS = 128
SB = 8
CAP = 4
GROUP = NX * NC
NJ = NY * NZ
CENTRE = 3.0
TILE = 8
POS, NRM, AREA = 0, 3, 6
ROWS, DOT, SQA, SQB, ONE = 16, 8, 9, 10, 11
KF, KS, KD = 32, 32, 48
VMEM_LIMIT = 16 << 20
UNROLL, TAIL = 32, 8
FLUX = SB * BS
LISTS = FLUX + SB * TILE
LANES = NYH * NZ


def contraction_terms():
    pieces = [(i, j) for i in range(3) for j in range(3) if i + j < 4]

    def product(scale, rrow, srow):
        return [
            (scale, i * ROWS + rrow + a, j * ROWS + srow + a) for i, j in pieces for a in range(3)
        ]

    def from_recv(row, count):
        return [(1.0, i * ROWS + row, ONE) for i in range(count)]

    def from_src(row, count):
        return [(1.0, ONE, i * ROWS + row) for i in range(count)]

    facing = product(1.0, NRM, POS) + from_recv(DOT, 3)
    seen = product(1.0, POS, NRM) + from_src(DOT, 3)
    cross = product(-2.0, POS, POS)
    spread = (
        from_src(SQA, 2) + from_recv(SQA, 2) + cross + from_recv(SQB, 3) + from_src(SQB, 3)
    )
    return (KF, facing), (KS, seen), (KD, spread)


def selections(side):
    made = []
    for depth, terms in contraction_terms():
        groups = []
        for start in range(0, depth, 8):
            row = lax.broadcasted_iota(jnp.int32, (8, 3 * ROWS), 0)
            column = lax.broadcasted_iota(jnp.int32, (8, 3 * ROWS), 1)
            group = jnp.zeros((8, 3 * ROWS), jnp.float32)
            for at, term in enumerate(terms[start : start + 8]):
                value = term[0] if side == 0 else 1.0
                here = (row == at) & (column == term[1 + side])
                group = jnp.where(here, value, group)
            groups.append(group)
        made.append(jnp.concatenate(groups, axis=0).astype(jnp.bfloat16))
    return made


def split_pieces(tile):
    row = lax.broadcasted_iota(jnp.int32, tile.shape, 0)
    fixed = row < NRM
    coarse = jnp.where(fixed, jnp.round(tile * 32.0) * (1.0 / 32.0), tile)
    along = -(
        tile[NRM : NRM + 1] * tile[POS : POS + 1]
        + tile[NRM + 1 : NRM + 2] * tile[POS + 1 : POS + 2]
        + tile[NRM + 2 : NRM + 3] * tile[POS + 2 : POS + 3]
    )
    grid = [coarse[a : a + 1] for a in range(3)]
    fine = [tile[a : a + 1] - grid[a] for a in range(3)]
    square_a = grid[0] * grid[0] + grid[1] * grid[1] + grid[2] * grid[2]
    square_b = (
        fine[0] * (2.0 * grid[0] + fine[0])
        + fine[1] * (2.0 * grid[1] + fine[1])
        + fine[2] * (2.0 * grid[2] + fine[2])
    ) + tile[AREA : AREA + 1]
    derived = jnp.where(
        row == 0,
        along,
        jnp.where(
            row == 1, square_a, jnp.where(row == 2, square_b, jnp.where(row == 3, 1.0, 0.0))
        ),
    )
    values = jnp.concatenate([tile, derived], axis=0)
    high = jnp.concatenate([coarse, derived], axis=0).astype(jnp.bfloat16)
    rest = values - high.astype(jnp.float32)
    cut = lax.broadcasted_iota(jnp.int32, values.shape, 0) < NRM
    mid = jnp.where(cut, jnp.round(rest * 8192.0) * (1.0 / 8192.0), rest).astype(jnp.bfloat16)
    low = (rest - mid.astype(jnp.float32)).astype(jnp.bfloat16)
    return jnp.concatenate([high, mid, low], axis=0)


def dot(a, b):
    return jnp.dot(a, b, preferred_element_type=jnp.float32)


def direction(angles):
    polar, azimuth = angles[0:1], angles[1:2]
    across = jnp.sin(polar)
    return [across * jnp.cos(azimuth), across * jnp.sin(azimuth), jnp.cos(polar)]


def pack_kernel(*refs):
    given, (packed, recv_tile), held, arrival = refs[:9], refs[9:11], refs[11:20], refs[20]
    copies = [
        pltpu.make_async_copy(source, target, arrival.at[at])
        for at, (source, target) in enumerate(zip(given, held))
    ]
    for copy in copies:
        copy.start()
    for copy in copies:
        copy.wait()
    incident, pos, angles, area, keep, lists, counts, recv_pos, recv_angles = held
    packed[:FLUX, :] = incident[...].astype(jnp.float32)
    scale = keep[...] * area[...] * (1.0 / np.pi)
    rows = [pos[a : a + 1, :] - CENTRE for a in range(3)]
    rows += [component * scale for component in direction(angles[...])]
    rows += [area[...], jnp.zeros_like(scale)]
    tile = jnp.concatenate(rows, axis=0)
    slot = lax.broadcasted_iota(jnp.int32, (CAP, LANES), 0)
    for k in range(SB):
        packed[FLUX + k * TILE : FLUX + (k + 1) * TILE, :] = tile[:, k * BS : (k + 1) * BS]
    for k in range(GROUP):
        for yl in range(NYL):
            slab = ((k // NC) * NYL + yl) * NC + k % NC
            live = slot < counts[slab : slab + 1, :]
            marked = jnp.where(live, lists[slab], -1).astype(jnp.float32)
            for c in range(CAP):
                at = (yl * CAP + c) * LANES
                packed[LISTS + k : LISTS + k + 1, at : at + LANES] = marked[c : c + 1, :]
    rows = [recv_pos[a : a + 1, :] - CENTRE for a in range(3)]
    rows += direction(recv_angles[...])
    rows += [jnp.zeros((2, BS), jnp.float32)]
    tile = jnp.concatenate(rows, axis=0)
    for j in range(NJ):
        recv_tile[j] = tile


def own_y():
    return lax.axis_index("yh") * NYL + lax.axis_index("yl")


def own_list():
    return lax.axis_index("x") * NC + lax.axis_index("c")


def src_prep_kernel(count, *refs):
    packed = refs[:count]
    sf, ss, sd, em, lists = refs[count:]
    mats = selections(1)
    for d, ref in enumerate(packed):
        for k in range(SB):
            em[d * SB + k] = ref[k * BS : (k + 1) * BS, :].astype(jnp.bfloat16)
        tiles = [ref[FLUX + k * TILE : FLUX + (k + 1) * TILE, :] for k in range(SB)]
        q = split_pieces(jnp.concatenate(tiles, axis=1))
        lists[d : d + 1, :] = ref[pl.ds(LISTS + own_list(), 1), :].astype(jnp.int32)
        for m, out in zip(mats, (sf, ss, sd)):
            values = dot(m, q).astype(jnp.bfloat16)
            for k in range(SB):
                out[d * SB + k] = values[:, k * BS : (k + 1) * BS]
    null = count * SB
    em[null] = jnp.zeros((BS, BS), jnp.bfloat16)
    sf[null] = jnp.zeros((KF, BS), jnp.bfloat16)
    ss[null] = jnp.zeros((KS, BS), jnp.bfloat16)
    first_row = lax.broadcasted_iota(jnp.int32, (KD, BS), 0) == 0
    sd[null] = jnp.where(first_row, 1.0, 0.0).astype(jnp.bfloat16)


def recv_prep_kernel(tiles, rf, rs, rd):
    mats = selections(0)
    for j in range(NJ):
        q = split_pieces(tiles[j])
        for m, ref in zip(mats, (rf, rs, rd)):
            ref[j] = lax.dot_general(
                q, m, (((0,), (1,)), ((), ())), preferred_element_type=jnp.float32
            ).astype(jnp.bfloat16)


def sweep_kernel(count, distances, added, sizes, lists, rf, rs, rd, sf, ss, sd, em, *refs):
    before, outs = refs[:added], refs[added:-3]
    out, ids, owner = refs[-3:]
    if len(sizes) == 1:
        out = outs[0]
    blocks = len(distances) * NZ
    null = sf.shape[0] - 1
    slots = count * CAP // 2

    def block_of(j):
        ahead = distances[0]
        for at in range(1, len(distances)):
            ahead = jnp.where(j >= at * NZ, distances[at], ahead)
        target = (own_y() + ahead) & (NY - 1)
        return ((target & (NYL - 1)) * NYH + (target >> 1)) * NZ + (j & (NZ - 1))

    for j in range(blocks):
        start = jnp.zeros((BS, BS), jnp.float32)
        if added:
            start = before[0][(distances[j // NZ] - 1) * NZ + j % NZ]
        out[j] = start

    def one_block(j, n):
        block = block_of(j)
        lane = (block >> 4) * CAP * LANES + (block & (LANES - 1))
        for t in range(slots):
            owner[n // 2 + t] = j
        for d in range(count):
            used = []
            for c in range(CAP):
                value = lists[d, lane + c * LANES]
                ids[n + c] = d * SB + value
                used.append((value >= 0).astype(jnp.int32))
            n = n + ((used[0] + used[1]) + (used[2] + used[3]))
        ids[n] = null
        return n + n % 2

    n = lax.fori_loop(0, blocks, one_block, 0)
    for t in range(2 * TAIL):
        ids[n + t] = null
    for t in range(TAIL):
        owner[n // 2 + t] = 0

    def front(u):
        a, b = ids[2 * u], ids[2 * u + 1]
        j = block_of(owner[u])

        def pair(ref):
            return jnp.concatenate([ref[a], ref[b]], axis=1)

        facing = jnp.maximum(dot(rf[j], pair(sf)), 0.0)
        seen = jnp.maximum(dot(rs[j], pair(ss)), 0.0)
        spread = dot(rd[j], pair(sd))
        return (facing * seen / (spread * spread)).astype(jnp.bfloat16)

    def back(u, values):
        a, b = ids[2 * u], ids[2 * u + 1]
        j = owner[u]
        out[j] = out[j] + dot(values, jnp.concatenate([em[a], em[b]], axis=0))

    def run(first_unit, width, steps):
        def step(i, carry):
            units = [first_unit + i * width + r for r in range(width)]
            values = [front(u) for u in units]
            for u, value in zip(units, values):
                back(u, value)
            return carry

        lax.fori_loop(0, steps, step, 0)

    units = n // 2
    long = units // UNROLL
    run(0, UNROLL, long)
    run(long * UNROLL, TAIL, pl.cdiv(units - long * UNROLL, TAIL))
    if len(sizes) > 1:
        at = 0
        for ref, size in zip(outs, sizes):
            ref[...] = out[at : at + size]
            at += size


VMEM_SPEC = pl.BlockSpec(memory_space=pltpu.VMEM)
SMEM_SPEC = pl.BlockSpec(memory_space=pltpu.SMEM)
BF16 = jnp.bfloat16
PARAMS = pltpu.CompilerParams(vmem_limit_bytes=VMEM_LIMIT)


def bf16_shape(*shape):
    return jax.ShapeDtypeStruct(shape, BF16)


def src_prep(packed):
    count = len(packed)
    rows = count * SB + 1
    return pl.pallas_call(
        functools.partial(src_prep_kernel, count),
        out_shape=[
            bf16_shape(rows, KF, BS),
            bf16_shape(rows, KS, BS),
            bf16_shape(rows, KD, BS),
            bf16_shape(rows, BS, BS),
            jax.ShapeDtypeStruct((count, BS), jnp.int32),
        ],
        in_specs=[VMEM_SPEC] * count,
        out_specs=[VMEM_SPEC] * 5,
        name="src_prep",
        compiler_params=PARAMS,
        cost_estimate=pl.CostEstimate(flops=10**6, bytes_accessed=10**6, transcendentals=0),
    )(*packed)


def recv_prep(tiles):
    return pl.pallas_call(
        recv_prep_kernel,
        out_shape=[bf16_shape(NJ, BS, KF), bf16_shape(NJ, BS, KS), bf16_shape(NJ, BS, KD)],
        in_specs=[VMEM_SPEC],
        out_specs=[VMEM_SPEC] * 3,
        name="recv_prep",
        compiler_params=PARAMS,
        cost_estimate=pl.CostEstimate(flops=10**6, bytes_accessed=10**6, transcendentals=0),
    )(tiles)


def sweep(distances, recv, src, count, *before, sizes=None):
    *src, lists = src
    blocks = len(distances) * NZ
    sizes = sizes or (blocks,)
    return pl.pallas_call(
        functools.partial(sweep_kernel, count, distances, len(before), sizes),
        out_shape=[jax.ShapeDtypeStruct((size, BS, BS), jnp.float32) for size in sizes],
        in_specs=[SMEM_SPEC] + [VMEM_SPEC] * (7 + len(before)),
        out_specs=[VMEM_SPEC] * len(sizes),
        scratch_shapes=[
            pltpu.VMEM((blocks if len(sizes) > 1 else 1, BS, BS), jnp.float32),
            pltpu.SMEM((blocks * count * CAP + 4 * UNROLL,), jnp.int32),
            pltpu.SMEM((blocks * count * CAP // 2 + count * CAP + 2 * UNROLL,), jnp.int32),
        ],
        name="sweep",
        compiler_params=PARAMS,
        cost_estimate=pl.CostEstimate(flops=10**6, bytes_accessed=10**6, transcendentals=0),
    )(lists, *recv, *src, *before)


def pack(*operands):
    return pl.pallas_call(
        pack_kernel,
        out_shape=[
            jax.ShapeDtypeStruct((LISTS + TILE, BS), jnp.float32),
            jax.ShapeDtypeStruct((NJ, 8, BS), jnp.float32),
        ],
        in_specs=[pl.BlockSpec(memory_space=pltpu.HBM)] * 9,
        out_specs=[VMEM_SPEC] * 2,
        scratch_shapes=[pltpu.VMEM(array.shape, array.dtype) for array in operands]
        + [pltpu.SemaphoreType.DMA((9,))],
        name="pack",
        compiler_params=PARAMS,
        cost_estimate=pl.CostEstimate(flops=10**6, bytes_accessed=10**6, transcendentals=0),
    )(*[pltpu.with_memory_space_constraint(array, pltpu.HBM) for array in operands])


def y_route(distance):
    def linear(y):
        return (y % NYL) * NYH + y // NYL

    return [(linear(y), linear((y + distance) % NY)) for y in range(NY)]


def shards(
    recv_pos,
    recv_angles,
    src_pos,
    src_angles,
    src_area,
    reemission,
    incident,
    direct,
    visible_lists,
    visible_counts,
):
    mine, recv_tile = pack(
        incident,
        src_pos,
        src_angles,
        src_area.reshape(1, SB * BS),
        reemission.reshape(1, SB * BS),
        visible_lists[0, 0].transpose(0, 2, 1),
        visible_counts[0, 0],
        recv_pos,
        recv_angles,
    )

    def along_x(block, distance):
        return lax.ppermute(block, "x", [(i, (i + distance) % NX) for i in range(NX)])

    def other_core(block):
        return lax.ppermute(block, "c", [(0, 1), (1, 0)])

    far = [along_x(mine, distance) for distance in (1, 3, 2)]
    own = other_core(mine)

    tiles = lax.all_to_all(recv_tile, ("yl", "yh", "z"), 0, 0, tiled=True)

    own, tiles = lax.optimization_barrier((own, tiles))
    recv = recv_prep(tiles)
    (begun,) = sweep((1, 2, 3), recv, src_prep([mine, own]), 2)
    *far, begun = lax.optimization_barrier((*far, begun))
    src = src_prep(far + [other_core(block) for block in far] + [mine, own])

    def along_y(block, distance):
        return lax.ppermute(block, ("yl", "yh"), y_route(distance))

    half = NZ // 2
    parts = sweep((2,), recv, src, GROUP - 2, begun, sizes=(half, half))
    by_left, by_right = along_y(parts[0], 1), along_y(parts[1], 3)
    ahead, behind = sweep((1, 3), recv, src, GROUP - 2, begun, sizes=(NZ, NZ))
    ahead = along_y(ahead.at[:half].add(by_left), 1)
    behind = along_y(behind.at[half:].add(by_right), 3)
    (total,) = sweep((0,), recv, src, GROUP)
    total = total + ahead + behind
    pieces = lax.all_to_all(total, "z", 0, 0, tiled=True)
    return direct + jnp.sum(pieces, axis=0)


def solution(mesh):
    fine = Mesh(mesh.devices.reshape(NX, NYL, NC, NYH, NZ), ("x", "yl", "c", "yh", "z"))
    blk, lane = ("x", "yl", "c"), ("yh", "z")
    both = blk + lane
    return jax.shard_map(
        shards,
        mesh=fine,
        in_specs=(
            P(None, both),
            P(None, both),
            P(None, both),
            P(None, both),
            P(both),
            P(both),
            P(both, None),
            P(both, None),
            P(blk, lane, None, None, None),
            P(blk, lane, None, None),
        ),
        out_specs=P(both, None),
        check_vma=False,
    )
```
